32 devices in a mesh: dp: 2 (over y), lat: 4 (over x, core), lon: 4 (over z).
Axes of the slice: x: 2, y: 2, z: 4, core: 2. Of those that a mesh axis runs over, the one named last changes fastest.
Arguments:
- fields: bfloat16 [2, 32, 64, 1024], P('dp', 'lat', 'lon'), may hold values from -6 to 6
- cotangent: bfloat16 [2, 32, 64, 512], P('dp', 'lat', 'lon'), may hold values from -6 to 6
- query_weight: bfloat16 [1024, 512], replicated, may hold values from -0.1875 to 0.1875
- keyval_weight: bfloat16 [1024, 1024], replicated, may hold values from -0.1875 to 0.1875
- position_bias: float32 [8, 13, 13], replicated, may hold values from -4 to 4
- land_bias: float32 [8], replicated, may hold values from -2 to 2
- valid_cell: int32 [32, 64], replicated, may hold values 0 or 1
- land_sea: int32 [32, 64], replicated, may hold values 0 or 1
Outputs:
- field_grad: bfloat16 [2, 32, 64, 1024], P('dp', 'lat', 'lon')
- keyval_grad: float32 [1024, 1024], P(('dp', 'lat', 'lon'))
The draws below stay inside these ranges and needn't reach their ends.
All inputs are finite; a program needn't handle non-finite values.
Results may differ from the reference program's by a relative error of at most 0.011.
Values may be sent and summed in bfloat16 or wider, within the bound.
A program may use at most 128 MiB of HBM per device.

```python
import jax
import jax.numpy as jnp
from jax import lax

D = 1024
HEADS = 8
WIN = 13
RLAT = 8
RLON = 16
QW = 512
HALO = 6
MEMBERS = 2
LAT_ALL = 32
LON_ALL = 64


def with_ends(drawn, stream_key, smallest, high):
    shape = drawn.shape
    place = [jax.random.randint(jax.random.fold_in(stream_key, axis), (), 0, shape[axis]) for axis in range(len(shape))]
    drawn = drawn.at[tuple(place)].set(smallest)
    longest = shape.index(max(shape))
    place[longest] = (place[longest] + 1) % shape[longest]
    return drawn.at[tuple(place)].set(high)


def steps_of(key, extent, cuts, smallest, top_value):
    factor_of, own = 1.0, jax.random.fold_in(key, 6)
    for dim, blocks in cuts:
        steps = jnp.exp(jax.random.uniform(jax.random.fold_in(own, dim), (blocks,), jnp.float32, smallest / len(cuts), top_value / len(cuts)))
        factor_of = factor_of * jnp.repeat(steps, extent[dim] // blocks).reshape([-1 if axis == dim else 1 for axis in range(len(extent))])
    return factor_of


def normal_values(rng, dims, scale, reach, pieces=(), held_as=jnp.bfloat16):
    array = scale * jax.random.normal(rng, dims, jnp.float32)
    if pieces:
        array = array * steps_of(rng, dims, pieces, -0.22, 0.18)
    return jnp.clip(array, -reach, reach).astype(held_as)


def setup_inputs(seed: int = 0) -> dict:
    key_list = jax.random.split(jax.random.key(seed), 9)
    return {
        "fields": normal_values(key_list[0], (MEMBERS, LAT_ALL, LON_ALL, D), 1.0, 6.0, ((0, 2), (1, 4), (2, 4))),
        "cotangent": normal_values(key_list[1], (MEMBERS, LAT_ALL, LON_ALL, QW), 1.0, 6.0, ((0, 2), (1, 4), (2, 4))),
        "query_weight": normal_values(key_list[2], (D, QW), D ** -0.5, 0.1875),
        "keyval_weight": normal_values(key_list[3], (D, 2 * QW), D ** -0.5, 0.1875),
        "position_bias": normal_values(key_list[4], (HEADS, WIN, WIN), 1.0, 4.0, (), jnp.float32),
        "land_bias": jnp.clip(jax.random.uniform(key_list[5], (HEADS,), jnp.float32, -2.0, 2.0), -2.0, 2.0),
        "valid_cell": with_ends((jax.random.randint(key_list[6], (LAT_ALL, LON_ALL), 0, 8) < 7).astype(jnp.int32), jax.random.fold_in(key_list[6], 1), 0, 1),
        "land_sea": with_ends((jax.random.randint(key_list[7], (LAT_ALL, LON_ALL), 0, 10) < 3).astype(jnp.int32), jax.random.fold_in(key_list[7], 1), 0, 1),
    }


CAP = 20.0


def offset_tables(n_query, n_key, shift):
    query_idx = jnp.arange(n_query)[:, None]
    key_idx = jnp.arange(n_key)[None, :]
    offset = key_idx - query_idx + shift
    inside = ((offset >= 0) & (offset < WIN)).astype(jnp.float32)
    onehot = (offset[:, :, None] == jnp.arange(WIN)[None, None, :]).astype(jnp.float32)
    centre = (offset == HALO).astype(jnp.float32)
    return inside, onehot, centre


def score_terms(position_bias, land_bias, land_key, key_ok, row_tab, col_tab, query_ok):
    row_in, row_hot, row_mid = row_tab
    col_in, col_hot, col_mid = col_tab
    partial_bias = jnp.einsum('hab,cxb->hacx', position_bias, col_hot, precision=lax.Precision.HIGHEST)
    full_bias = jnp.einsum('hacx,rya->hrcyx', partial_bias, row_hot, precision=lax.Precision.HIGHEST)
    n_query = row_hot.shape[0] * col_hot.shape[0]
    n_key = row_hot.shape[1] * col_hot.shape[1]
    full_bias = full_bias.reshape(position_bias.shape[0], n_query, n_key)
    window = row_in[:, None, :, None] * col_in[None, :, None, :]
    centre = row_mid[:, None, :, None] * col_mid[None, :, None, :]
    allowed = window * jnp.maximum(key_ok[None, None], centre) * query_ok[:, :, None, None]
    land_term = land_bias[:, None, None] * land_key.reshape(1, 1, n_key)
    return full_bias + land_term, allowed.reshape(n_query, n_key)


def block_pass(query_blk, keyval_blk, dout_blk, key_ok, land_key, position_bias, land_bias):
    band_rows, sector_cols, q_width = query_blk.shape
    ext_rows, ext_cols = band_rows + 2 * HALO, sector_cols + 2 * HALO
    n_query = band_rows * sector_cols
    n_key = ext_rows * ext_cols
    heads_count = position_bias.shape[0]
    head_size = q_width // heads_count
    scale = head_size ** -0.5
    row_tab = offset_tables(band_rows, ext_rows, 0)
    col_tab = offset_tables(sector_cols, ext_cols, 0)
    query_ok = jnp.ones((band_rows, sector_cols), jnp.float32)
    bias, allowed = score_terms(position_bias, land_bias, land_key, key_ok, row_tab, col_tab, query_ok)
    query4 = query_blk.reshape(n_query, heads_count, head_size).astype(jnp.float32)
    flat_kv = keyval_blk.reshape(n_key, 2 * q_width)
    key4 = flat_kv[:, :q_width].reshape(n_key, heads_count, head_size).astype(jnp.float32)
    value4 = flat_kv[:, q_width:].reshape(n_key, heads_count, head_size).astype(jnp.float32)
    dout4 = dout_blk.reshape(n_query, heads_count, head_size).astype(jnp.float32)
    raw = jnp.einsum('qhd,khd->hqk', query4, key4) * scale + bias
    capped = CAP * jnp.tanh(raw / CAP)
    expd = jnp.exp(capped) * allowed[None]
    denom = jnp.sum(expd, axis=-1, keepdims=True)
    weight = expd / denom
    weight_b = weight.astype(jnp.bfloat16)
    dots = jnp.einsum('qhd,khd->hqk', dout4, value4)
    delta = jnp.sum(weight * dots, axis=-1, keepdims=True)
    dscore = (weight * (dots - delta) * (1.0 - (capped / CAP) ** 2) * scale).astype(jnp.bfloat16)
    dscore_f = dscore.astype(jnp.float32)
    query_grad = jnp.einsum('hqk,khd->qhd', dscore_f, key4).astype(jnp.bfloat16).reshape(band_rows, sector_cols, q_width)
    key_grad = jnp.einsum('hqk,qhd->khd', dscore_f, query4).reshape(n_key, q_width)
    value_grad = jnp.einsum('hqk,qhd->khd', weight_b.astype(jnp.float32), dout4).reshape(n_key, q_width)
    both = jnp.concatenate([key_grad, value_grad], axis=-1).reshape(ext_rows, ext_cols, 2 * q_width)
    return query_grad, both


def widen(grid):
    padded = jnp.pad(grid, ((HALO, HALO), (0, 0)) + ((0, 0),) * (grid.ndim - 2))
    return jnp.concatenate([padded[:, -HALO:], padded, padded[:, :HALO]], axis=1)


def member_pass(field_mem, dout_mem, query_weight, keyval_weight, position_bias, land_bias, key_ok_ext, land_ext):
    lat_all, lon_all, width = field_mem.shape
    q_width = query_weight.shape[1]
    flat = field_mem.reshape(lat_all * lon_all, width)
    queries = jnp.dot(flat, query_weight, preferred_element_type=jnp.float32).astype(jnp.bfloat16).reshape(lat_all, lon_all, q_width)
    keyvals = jnp.dot(flat, keyval_weight, preferred_element_type=jnp.float32).astype(jnp.bfloat16).reshape(lat_all, lon_all, 2 * q_width)
    keyval_ext = widen(keyvals)
    blocks_lon = lon_all // RLON
    blocks_all = (lat_all // RLAT) * blocks_lon
    zero = jnp.zeros((), jnp.int32)
    grad_ext = jnp.zeros((lat_all + 2 * HALO, lon_all + 2 * HALO, 2 * q_width), jnp.float32)
    query_all = jnp.zeros((lat_all, lon_all, q_width), jnp.bfloat16)

    def step(index, carry):
        grad_acc, query_acc = carry
        index = jnp.asarray(index).astype(jnp.int32)
        row_start = ((index // blocks_lon) * RLAT).astype(jnp.int32)
        col_start = ((index % blocks_lon) * RLON).astype(jnp.int32)
        query_blk = lax.dynamic_slice(queries, (row_start, col_start, zero), (RLAT, RLON, q_width))
        dout_blk = lax.dynamic_slice(dout_mem, (row_start, col_start, zero), (RLAT, RLON, q_width))
        keyval_blk = lax.dynamic_slice(keyval_ext, (row_start, col_start, zero), (RLAT + 2 * HALO, RLON + 2 * HALO, 2 * q_width))
        ok_blk = lax.dynamic_slice(key_ok_ext, (row_start, col_start), (RLAT + 2 * HALO, RLON + 2 * HALO))
        land_blk = lax.dynamic_slice(land_ext, (row_start, col_start), (RLAT + 2 * HALO, RLON + 2 * HALO))
        query_grad, both = block_pass(query_blk, keyval_blk, dout_blk, ok_blk, land_blk, position_bias, land_bias)
        query_acc = lax.dynamic_update_slice(query_acc, query_grad, (row_start, col_start, zero))
        old = lax.dynamic_slice(grad_acc, (row_start, col_start, zero), both.shape)
        grad_acc = lax.dynamic_update_slice(grad_acc, old + both, (row_start, col_start, zero))
        return grad_acc, query_acc

    grad_ext, query_all = lax.fori_loop(0, blocks_all, step, (grad_ext, query_all))
    inner = grad_ext[HALO:-HALO]
    core = inner[:, HALO:-HALO]
    core = core.at[:, :HALO].add(inner[:, -HALO:])
    core = core.at[:, -HALO:].add(inner[:, :HALO])
    keyval_cell = core.astype(jnp.bfloat16).reshape(lat_all * lon_all, 2 * q_width)
    query_flat = query_all.reshape(lat_all * lon_all, q_width)
    field_grad = jnp.dot(query_flat, query_weight.T, preferred_element_type=jnp.float32) + jnp.dot(keyval_cell, keyval_weight.T, preferred_element_type=jnp.float32)
    weight_part = jnp.dot(flat.T, keyval_cell, preferred_element_type=jnp.float32)
    return field_grad.astype(jnp.bfloat16).reshape(lat_all, lon_all, width), weight_part


def reference(fields, cotangent, query_weight, keyval_weight, position_bias, land_bias, valid_cell, land_sea):
    key_ok_ext = widen(valid_cell.astype(jnp.float32))
    land_ext = widen(land_sea.astype(jnp.float32))

    def one_member(pair):
        return member_pass(pair[0], pair[1], query_weight, keyval_weight, position_bias, land_bias, key_ok_ext, land_ext)

    field_grad, weight_parts = lax.map(one_member, (fields, cotangent))
    total = fields.shape[0] * fields.shape[1] * fields.shape[2]
    keyval_grad = jnp.sum(weight_parts, axis=0) * (float(total) ** -0.5)
    return field_grad, keyval_grad
```

```python
import jax
import jax.numpy as jnp
from jax import lax
from jax.experimental import pallas as pl
from jax.experimental.pallas import tpu as pltpu
from jax.sharding import PartitionSpec as P

CAP = 20.0
MESH = pl.DeviceIdType.MESH
F32, BF16 = jnp.float32, jnp.bfloat16
OCT = 8
NEAR = (((1,), (1,)), ((), ()))
TALL = (((0,), (0,)), ((), ()))


class Plan:
    def __init__(self, rows, cols, reach, heads, size, lat, lon, dp):
        self.rows, self.cols, self.reach, self.heads, self.size = rows, cols, reach, heads, size
        self.lat, self.lon, self.dp = lat, lon, dp
        self.nq = rows * cols
        self.ext = rows + 2 * reach
        self.octets = cols // OCT + 2
        self.per_oct = self.ext * OCT
        self.nk = self.octets * self.per_oct
        self.half = rows * OCT
        self.groups = heads // 2
        self.edge = reach * OCT
        self.regions = []
        last = self.octets - 1
        for o in range(self.octets):
            for part in (-1, 0, 1):
                step = -1 if o == 0 else (1 if o == last else 0)
                if step == 0 and part == 0:
                    continue
                owner = last - 1 if o == 0 else (1 if o == last else o)
                start = (self.half - self.edge) if part == -1 else 0
                count = self.half if part == 0 else self.edge
                at = o * self.per_oct + (0 if part == -1 else self.edge + (0 if part == 0 else self.half))
                self.regions.append((step, part, owner, start, count, at))
        self.group_all = dp == 2 and lat == 4

    def own_at(self, o):
        return o * self.per_oct + self.edge


def body(pn, scale, norm, refs):
    (f_ref, d_ref, wq_ref, wkv_ref, lines_ref, land_bias_ref, valid_ref, land_ref) = refs[:8]
    if pn.group_all:
        fg_out, kv_out = refs[8:10]
        rest = refs[10:]
    else:
        fg_out, cell_out = refs[8:10]
        rest = refs[10:]
    (ext, gsend, grecv, own, q2, do2, bias, okay, dq_s, hs, hr, gs, gr) = rest[:13]
    if pn.group_all:
        (fall, cell, kall, zsend, zrecv, fsum, ocol, fs, fr, ks, kr, zs, zr, os_, or_) = rest[13:]
    lat, lon, dp = lax.axis_index("lat"), lax.axis_index("lon"), lax.axis_index("dp")
    nlat, nlon = pn.lat, pn.lon
    hd = pn.size
    gw = 2 * hd
    qw = pn.heads * hd

    def at(dlat, dlon, ddp=0):
        return (
            lax.rem(dp + ddp, pn.dp) if ddp else dp,
            lax.rem(lat + dlat + nlat, nlat) if dlat else lat,
            lax.rem(lon + dlon + nlon, nlon) if dlon else lon,
        )

    peers = [(0, a, b) for a in (-1, 0, 1) for b in (-1, 0, 1) if a or b]
    if pn.group_all:
        steps = [(d, a, 0) for d in range(2) for a in range(-1, 3) if d or a]
        steps += [(0, 0, b) for b in range(1, nlon)]
        for d, a, b in steps:
            seen = {(u, v % nlat, w % nlon) for u, v, w in peers}
            if (d, a % nlat, b % nlon) not in seen:
                peers.append((d, a, b))
    barrier = pltpu.get_barrier_semaphore()
    for d, a, b in peers:
        pl.semaphore_signal(barrier, inc=1, device_id=at(a, b, d), device_id_type=MESH)
    pl.semaphore_wait(barrier, len(peers))

    def remote(src, dst, ssem, rsem, dev):
        return pltpu.make_async_remote_copy(
            src_ref=src, dst_ref=dst, send_sem=ssem, recv_sem=rsem, device_id=dev, device_id_type=MESH
        )

    def halo(g, i):
        step, part, owner, start, count, where = pn.regions[i]
        return remote(
            ext.at[g, pl.ds(pn.own_at(owner) + start, count)],
            ext.at[g, pl.ds(where, count)],
            hs.at[g, i], hr.at[g, i], at(-part, -step),
        )

    def back(g, i):
        step, part, owner, start, count, where = pn.regions[i]
        return remote(
            gsend.at[g, pl.ds(where, count)],
            grecv.at[g, pl.ds(where, count)],
            gs.at[g, i], gr.at[g, i], at(part, step),
        )

    nreg = len(pn.regions)

    flat = f_ref[...]
    for g in range(pn.groups):
        for kv in range(2):
            w = wkv_ref[:, kv * qw + g * gw : kv * qw + (g + 1) * gw]
            got = jnp.dot(flat, w, preferred_element_type=F32)
            got = got.reshape(pn.rows, pn.cols // OCT, OCT, gw)
            for o in range(1, pn.octets - 1):
                ext[g, pl.ds(pn.own_at(o), pn.half), kv * gw : (kv + 1) * gw] = (
                    got[:, o - 1].reshape(pn.half, gw).astype(BF16)
                )
        for i in range(nreg):
            halo(g, i).start()

    if pn.group_all:
        slot = dp * 4 + lat
        fall[slot] = flat

        def flip(kind):
            return ((1 - dp, lat, lon), (dp, lax.rem(lat + 2, 4), lon), (dp, lat + 1 - 2 * lax.rem(lat, 2), lon))[kind]

        def slot_of(ddp, dx):
            return (dp + ddp - 2 * dp * ddp) * 4 + lax.rem(lat + 2 * dx, 4)

        hops = [(0, 0, 0), (1, 0, 0), (2, 0, 0), (1, 1, 0), (2, 1, 0), (2, 0, 1), (2, 1, 1)]

        def hop(n):
            kind, ddp, dx = hops[n]
            s = slot_of(ddp, dx)
            return remote(fall.at[s], fall.at[s], fs.at[n], fr.at[n], flip(kind))

        def hop_in(n):
            kind, ddp, dx = hops[n]
            if kind == 0:
                s = slot_of(1 - ddp, dx)
            elif kind == 1:
                s = slot_of(ddp, 1 - dx)
            else:
                mate = lat + 1 - 2 * lax.rem(lat, 2)
                s = (dp + ddp - 2 * dp * ddp) * 4 + lax.rem(mate + 2 * dx, 4)
            return remote(fall.at[s], fall.at[s], fs.at[n], fr.at[n], flip(kind))

        for n in (0, 1, 2):
            hop(n).start()

    lane = lax.broadcasted_iota(jnp.int32, (pn.nq, gw), 1)
    for g in range(pn.groups):
        got = jnp.dot(flat, wq_ref[:, g * gw : (g + 1) * gw], preferred_element_type=F32)
        dout = d_ref[:, g * gw : (g + 1) * gw].astype(F32)
        for hh in range(2):
            mine = (lane < hd) if hh == 0 else (lane >= hd)
            q2[g, hh * pn.nq : (hh + 1) * pn.nq] = jnp.where(mine, got, 0.0).astype(BF16)
            do2[g, hh * pn.nq : (hh + 1) * pn.nq] = jnp.where(mine, dout, 0.0).astype(BF16)

    nlat_all, nlon_all = valid_ref.shape

    def parts_of(n):
        shape = (pn.octets, pn.ext, OCT, n)
        o, row, c = (lax.broadcasted_iota(jnp.int32, shape, k).reshape(pn.nk, n) for k in range(3))
        return o * OCT + c, row, lax.broadcasted_iota(jnp.int32, (pn.nk, n), 1)

    col, row, li = parts_of(nlat_all)
    pick_row = jnp.where(li == row - pn.reach + lat * pn.rows, 1.0, 0.0).astype(BF16)
    col, row, li = parts_of(nlon_all)
    here = col - OCT + lon * pn.cols
    here = jnp.where(here < 0, here + nlon_all, here)
    here = jnp.where(here >= nlon_all, here - nlon_all, here)
    pick_col = li == here
    ones = jnp.ones((nlon_all, pn.nq), BF16)

    def key_values(ref):
        rows_of = jnp.dot(pick_row, ref[...].astype(F32).astype(BF16), preferred_element_type=F32)
        return jnp.dot(jnp.where(pick_col, rows_of, 0.0).astype(BF16), ones, preferred_element_type=F32)

    land = key_values(land_ref)
    ok = key_values(valid_ref)
    col, row, li = parts_of(pn.nq)
    a = row - li // pn.cols
    b = col - OCT + pn.reach - li % pn.cols
    side = 2 * pn.reach
    inside = (a >= 0) & (a <= side) & (b >= 0) & (b <= side)
    centre = (a == pn.reach) & (b == pn.reach)
    okay[...] = jnp.where(inside, jnp.where(centre, 1.0, ok), 0.0)
    per = pn.nq // pn.cols
    for g in range(pn.groups):
        for hh in range(2):
            h = 2 * g + hh
            for o in range(pn.octets):
                line = lines_ref[h, o]
                width = line.shape[1]
                for k in range(min(per, pn.ext)):
                    turned = line if k == 0 else pltpu.roll(line, width - k * pn.cols, 1)
                    for m in range((pn.ext - 1) // per + 1):
                        r = pn.ext - 1 - (m * per + k)
                        if r < 0:
                            continue
                        first = (o * pn.ext + r) * OCT
                        bias[g, first : first + OCT, hh * pn.nq : (hh + 1) * pn.nq] = (
                            turned[:, m * pn.nq : (m + 1) * pn.nq]
                            + land_bias_ref[h] * land[first : first + OCT]
                        )

    def step(g, carry):
        for i in range(nreg):
            halo(g, i).wait_recv()
        key = ext[g, :, 0:gw]
        value = ext[g, :, gw : 2 * gw]
        qg, dg = q2[g], do2[g]
        raw = lax.dot_general(key, qg, NEAR, preferred_element_type=F32) * scale + bias[g]
        dots = lax.dot_general(value, dg, NEAR, preferred_element_type=F32)
        bent = jnp.tanh(raw * (1.0 / CAP))
        ok1 = okay[...]
        expd = jnp.exp(CAP * bent) * jnp.concatenate([ok1, ok1], axis=1)
        weight = expd * (1.0 / jnp.sum(expd, axis=0, keepdims=True))
        delta = jnp.sum(weight * dots, axis=0, keepdims=True)
        ds = (weight * (dots - delta) * ((1.0 - bent * bent) * scale)).astype(BF16)
        wb = weight.astype(BF16)
        for kv, (left, right) in enumerate(((ds, qg), (wb, dg))):
            got = jnp.dot(left, right, preferred_element_type=F32)
            for o in range(1, pn.octets - 1):
                own[g, pl.ds((o - 1) * pn.half, pn.half), kv * gw : (kv + 1) * gw] = got[
                    pn.own_at(o) : pn.own_at(o) + pn.half
                ]
            gsend[g, :, kv * gw : (kv + 1) * gw] = got.astype(BF16)
        for i in range(nreg):
            back(g, i).start()
        turned = lax.dot_general(key, ds, TALL, preferred_element_type=F32)
        both = jnp.concatenate([turned[:hd, : pn.nq], turned[hd:, pn.nq :]], axis=0)
        dq_s[g] = both.T.astype(BF16)
        return carry

    if pn.group_all:
        lax.fori_loop(0, 1, step, 0)
        hop_in(0).wait_recv()
        hop(3).start()
        hop(4).start()
        lax.fori_loop(1, pn.groups - 1, step, 0)
        hop_in(1).wait_recv()
        hop(5).start()
        hop_in(3).wait_recv()
        hop(6).start()
        lax.fori_loop(pn.groups - 1, pn.groups, step, 0)
    else:
        lax.fori_loop(0, pn.groups, step, 0)

    dq = jnp.concatenate([dq_s[g] for g in range(pn.groups)], axis=1)
    first = lax.dot_general(dq, wq_ref[...], NEAR, preferred_element_type=F32)
    if pn.group_all:
        fsum[...] = first

        def kcopy(n, out):
            d, x = n // 4, n % 4
            tdp = lax.rem(dp + d, 2)
            tlat = lax.rem(lat + x, 4)
            fdp = lax.rem(dp + d, 2)
            flat_ = lax.rem(lat + 4 - x, 4)
            to = tdp * 4 + tlat
            frm = slot if out else fdp * 4 + flat_
            return remote(
                cell.at[to], kall.at[frm], ks.at[n], kr.at[n], (tdp, tlat, lon)
            )

        target = cell
    nat = pn.cols // OCT
    pieces = {}
    for g in range(pn.groups):
        for i in range(nreg):
            back(g, i).wait_recv()
        halves = []
        for o in range(1, pn.octets - 1):
            total = own[g, pl.ds((o - 1) * pn.half, pn.half)]
            for step_, part, owner, start, count, where in pn.regions:
                if owner != o:
                    continue
                add = grecv[g, pl.ds(where, count)].astype(F32)
                if count < pn.half:
                    zero = jnp.zeros((pn.half - count, add.shape[1]), F32)
                    add = jnp.concatenate([zero, add] if start else [add, zero], axis=0)
                total = total + add
            halves.append(total.reshape(pn.rows, 1, OCT, 2 * gw))
        full = jnp.concatenate(halves, axis=1).reshape(pn.nq, 2 * gw).astype(BF16)
        for kv in range(2):
            pieces[kv * pn.groups + g] = full[:, kv * gw : (kv + 1) * gw]
            if pn.group_all:
                cell[kv * pn.groups + g] = full[:, kv * gw : (kv + 1) * gw]
    if pn.group_all:
        for n in range(1, 8):
            kcopy(n, True).start()
    cells = jnp.concatenate([pieces[k] for k in range(2 * pn.groups)], axis=1)
    second = lax.dot_general(cells, wkv_ref[...], NEAR, preferred_element_type=F32)
    if not pn.group_all:
        cell_out[...] = cells
        fg_out[...] = (first + second).astype(BF16)
    else:
        fg_out[...] = (fsum[...] + second).astype(BF16)
        kall[slot] = cell[slot]
        for n in (2, 4, 5, 6):
            hop_in(n).wait_recv()
        for n in range(1, 8):
            kcopy(n, False).wait_recv()
        ka = kall[...].reshape(8 * pn.nq, gw)
        fa = fall[...].reshape(8 * pn.nq, fall.shape[2])
        grad = lax.dot_general(ka, fa, TALL, preferred_element_type=F32).T
        depth = grad.shape[0] // (8 * nlon)
        grad = (grad * norm).reshape(8, nlon, depth, gw)

        def zcopy(n):
            to = lax.rem(lon + n, nlon)
            return remote(zsend.at[to], zrecv.at[n - 1], zs.at[n - 1], zr.at[n - 1], (dp, lat, to))

        for z in range(nlon):
            zsend[z] = grad[:, z].reshape(8 * depth, gw).astype(BF16)
        for n in range(1, nlon):
            zcopy(n).start()
        for n in range(1, nlon):
            zcopy(n).wait_recv()
        total = zsend[lon].astype(F32)
        for n in range(1, nlon):
            total = total + zrecv[n - 1].astype(F32)
        ocol[...] = total.reshape(8, depth, gw)

        def ocopy(n, out):
            d, x = n // 4, n % 4
            tdp = lax.rem(dp + d, 2)
            tlat = lax.rem(lat + x, 4)
            frm = slot if out else tdp * 4 + lax.rem(lat + 4 - x, 4)
            where = pl.ds(pl.multiple_of(frm * gw, gw), gw)
            return remote(
                ocol.at[tdp * 4 + tlat], kv_out.at[:, where], os_.at[n], or_.at[n], (tdp, tlat, lon)
            )

        for n in range(1, 8):
            ocopy(n, True).start()
        kv_out[:, pl.ds(pl.multiple_of(slot * gw, gw), gw)] = ocol[slot]
        for n in range(1, 8):
            ocopy(n, False).wait_recv()
        for n in range(1, 8):
            kcopy(n, True).wait_send()
            ocopy(n, True).wait_send()
        for n in range(1, nlon):
            zcopy(n).wait_send()
        for n in range(7):
            hop(n).wait_send()
    for g in range(pn.groups):
        for i in range(nreg):
            halo(g, i).wait_send()
            back(g, i).wait_send()


def bias_lines(position_bias, pn):
    heads, side, _ = position_bias.shape
    lanes = 4 * pn.nq
    turns = lanes // pn.cols
    turned = jnp.flip(position_bias, axis=1)
    before = pn.ext - side
    turned = jnp.pad(turned, ((0, 0), (before, turns - before - side), (0, 0)))
    keys = pn.octets * OCT
    k = jnp.arange(keys)[None, :, None]
    c = jnp.arange(pn.cols)[None, None, :]
    hot = (jnp.arange(side)[:, None, None] == k - c + pn.reach - OCT).astype(F32)
    lines = jnp.einsum("htb,bkc->hktc", turned, hot, precision=lax.Precision.HIGHEST)
    return lines.reshape(heads, pn.octets, OCT, lanes)


def shards(
    fields, cotangent, query_weight, keyval_weight, position_bias, land_bias, valid_cell, land_sea
):
    rows, cols, width = fields.shape[1:]
    q_width = query_weight.shape[1]
    heads = position_bias.shape[0]
    size = q_width // heads
    reach = (position_bias.shape[1] - 1) // 2
    nlat, nlon, ndp = lax.axis_size("lat"), lax.axis_size("lon"), lax.axis_size("dp")
    pn = Plan(rows, cols, reach, heads, size, nlat, nlon, ndp)
    flat = fields.reshape(pn.nq, width)
    dout = cotangent.reshape(pn.nq, q_width)
    devices = nlat * nlon * ndp
    norm = float(pn.nq * devices) ** (-0.5)
    gw = 2 * size
    vm = pl.BlockSpec(memory_space=pltpu.VMEM)
    dma = pltpu.SemaphoreType.DMA
    nreg = len(pn.regions)
    g = pn.groups
    scratch = [
        pltpu.VMEM((g, pn.nk, 2 * gw), BF16),
        pltpu.VMEM((g, pn.nk, 2 * gw), BF16),
        pltpu.VMEM((g, pn.nk, 2 * gw), BF16),
        pltpu.VMEM((g, pn.nq, 2 * gw), F32),
        pltpu.VMEM((g, 2 * pn.nq, gw), BF16),
        pltpu.VMEM((g, 2 * pn.nq, gw), BF16),
        pltpu.VMEM((g, pn.nk, 2 * pn.nq), F32),
        pltpu.VMEM((pn.nk, pn.nq), F32),
        pltpu.VMEM((g, pn.nq, gw), BF16),
        dma((g, nreg)), dma((g, nreg)), dma((g, nreg)), dma((g, nreg)),
    ]
    out_shape = [jax.ShapeDtypeStruct((pn.nq, width), BF16)]
    if pn.group_all:
        depth = width // devices
        out_shape.append(jax.ShapeDtypeStruct((depth, 2 * q_width), F32))
        scratch += [
            pltpu.VMEM((8, pn.nq, width), BF16),
            pltpu.VMEM((8, pn.nq, gw), BF16),
            pltpu.VMEM((8, pn.nq, gw), BF16),
            pltpu.VMEM((nlon, 8 * depth, gw), BF16),
            pltpu.VMEM((nlon - 1, 8 * depth, gw), BF16),
            pltpu.VMEM((pn.nq, width), F32),
            pltpu.VMEM((8, depth, gw), F32),
            dma((7,)), dma((7,)), dma((8,)), dma((8,)),
            dma((nlon - 1,)), dma((nlon - 1,)), dma((8,)), dma((8,)),
        ]
    else:
        out_shape.append(jax.ShapeDtypeStruct((pn.nq, 2 * q_width), BF16))

    def kernel(*refs):
        body(pn, size ** (-0.5), norm, refs)

    field_grad, other = pl.pallas_call(
        kernel,
        out_shape=out_shape,
        in_specs=[vm] * 5 + [pl.BlockSpec(memory_space=pltpu.SMEM)] + [vm] * 2,
        out_specs=[vm, vm],
        scratch_shapes=scratch,
        name="attention_grads",
        compiler_params=pltpu.CompilerParams(
            collective_id=0, has_side_effects=True, vmem_limit_bytes=48 * 1024 * 1024
        ),
    )(
        flat, dout, query_weight, keyval_weight, bias_lines(position_bias, pn), land_bias,
        valid_cell, land_sea,
    )
    field_grad = field_grad.reshape(1, rows, cols, width)
    if pn.group_all:
        return field_grad, other
    term = lax.dot_general(flat, other, (((0,), (0,)), ((), ())), preferred_element_type=F32)
    keyval_grad = lax.psum_scatter(
        term * norm, ("dp", "lat", "lon"), scatter_dimension=0, tiled=True
    )
    return field_grad, keyval_grad


def solution(mesh):
    block = P("dp", "lat", "lon", None)
    in_specs = (block, block, P(), P(), P(), P(), P(), P())
    out_specs = (block, P(("dp", "lat", "lon"), None))
    return jax.shard_map(shards, mesh=mesh, in_specs=in_specs, out_specs=out_specs, check_vma=False)
```

```python
import jax
import jax.numpy as jnp
from jax import lax
from jax.experimental import pallas as pl
from jax.experimental.pallas import tpu as pltpu
from jax.sharding import PartitionSpec as P

CAP = 20.0
MESH = pl.DeviceIdType.MESH
F32, BF16 = jnp.float32, jnp.bfloat16
OCT = 8
NEAR = (((1,), (1,)), ((), ()))
TALL = (((0,), (0,)), ((), ()))


class Plan:
    def __init__(self, rows, cols, reach, heads, size, lat, lon, dp):
        self.rows, self.cols, self.reach, self.heads, self.size = rows, cols, reach, heads, size
        self.lat, self.lon, self.dp = lat, lon, dp
        self.nq = rows * cols
        self.ext = rows + 2 * reach
        self.octets = cols // OCT + 2
        self.per_oct = self.ext * OCT
        self.nk = self.octets * self.per_oct
        self.half = rows * OCT
        self.groups = heads // 2
        self.edge = reach * OCT
        self.regions = []
        last = self.octets - 1
        for o in range(self.octets):
            for part in (-1, 0, 1):
                step = (-1 if o == 0 else (1 if o == last else 0)) if part == 0 else 0
                if step == 0 and part == 0:
                    continue
                owner = (last - 1 if o == 0 else 1) if part == 0 else o
                start = (self.half - self.edge) if part == -1 else 0
                count = self.half if part == 0 else self.edge
                at = o * self.per_oct + (0 if part == -1 else self.edge + (0 if part == 0 else self.half))
                self.regions.append((step, part, owner, start, count, at))
        self.lon_ids = [i for i, r in enumerate(self.regions) if r[1] == 0]
        self.near_ids = [i for i, r in enumerate(self.regions) if r[1] and 0 < r[2] < last]
        self.corner_ids = [i for i, r in enumerate(self.regions) if r[1] and r[2] in (0, last)]
        self.lat_ids = self.near_ids + self.corner_ids
        self.group_all = dp == 2 and lat == 4

    def own_at(self, o):
        return o * self.per_oct + self.edge


def body(pn, scale, norm, refs):
    (f_ref, d_ref, wq_ref, wkv_ref, lines_ref, land_bias_ref, valid_ref, land_ref) = refs[:8]
    if pn.group_all:
        fg_out, kv_out = refs[8:10]
        rest = refs[10:]
    else:
        fg_out, cell_out = refs[8:10]
        rest = refs[10:]
    (ext, gsend, grecv, own, q2, do2, bias, okay, dq_s, hs, hr, gs, gr) = rest[:13]
    if pn.group_all:
        (fall, cell, kall, zsend, zrecv, fsum, ocol, fs, fr, ks, kr, zs, zr, os_, or_) = rest[13:]
    lat, lon, dp = lax.axis_index("lat"), lax.axis_index("lon"), lax.axis_index("dp")
    nlat, nlon = pn.lat, pn.lon
    hd = pn.size
    gw = 2 * hd
    qw = pn.heads * hd

    def at(dlat, dlon, ddp=0):
        return (
            lax.rem(dp + ddp, pn.dp) if ddp else dp,
            lax.rem(lat + dlat + nlat, nlat) if dlat else lat,
            lax.rem(lon + dlon + nlon, nlon) if dlon else lon,
        )

    peers = [(0, a, b) for a in (-1, 0, 1) for b in (-1, 0, 1) if (a == 0) != (b == 0)]
    if pn.group_all:
        steps = [(d, a, 0) for d in range(2) for a in range(-1, 3) if d or a]
        steps += [(0, 0, b) for b in range(1, nlon)]
        for d, a, b in steps:
            seen = {(u, v % nlat, w % nlon) for u, v, w in peers}
            if (d, a % nlat, b % nlon) not in seen:
                peers.append((d, a, b))
    barrier = pltpu.get_barrier_semaphore()
    for d, a, b in peers:
        pl.semaphore_signal(barrier, inc=1, device_id=at(a, b, d), device_id_type=MESH)
    pl.semaphore_wait(barrier, len(peers))

    def remote(src, dst, ssem, rsem, dev):
        return pltpu.make_async_remote_copy(
            src_ref=src, dst_ref=dst, send_sem=ssem, recv_sem=rsem, device_id=dev, device_id_type=MESH
        )

    def halo(g, i):
        step, part, owner, start, count, where = pn.regions[i]
        return remote(
            ext.at[g, pl.ds(pn.own_at(owner) + start, count)],
            ext.at[g, pl.ds(where, count)],
            hs.at[g, i], hr.at[g, i], at(-part, -step),
        )

    def back(g, i):
        step, part, owner, start, count, where = pn.regions[i]
        return remote(
            gsend.at[g, pl.ds(where, count)],
            grecv.at[g, pl.ds(where, count)],
            gs.at[g, i], gr.at[g, i], at(part, step),
        )

    def only(cond, act):
        if cond is None:
            act()
        else:
            pl.when(cond)(act)

    def below(part):
        return None if part == 0 else (lat < nlat - 1 if part == -1 else lat > 0)

    def above(part):
        return below(-part)

    def run(make, side, ids, g, what):
        for part in (-1, 0, 1):
            chosen = [i for i in ids if pn.regions[i][1] == part]
            if chosen:
                only(side(part), lambda: [getattr(make(g, i), what)() for i in chosen] and None)

    for part in (-1, 1):
        def clear(part=part):
            for g in range(pn.groups):
                for step, p, owner, start, count, where in pn.regions:
                    if p == part:
                        ext[g, pl.ds(where, count)] = jnp.zeros((count, 2 * gw), BF16)
                    if p == -part:
                        grecv[g, pl.ds(where, count)] = jnp.zeros((count, 2 * gw), BF16)

        pl.when(lat == (0 if part == -1 else nlat - 1))(clear)

    flat = f_ref[...]
    for g in range(pn.groups):
        for kv in range(2):
            w = wkv_ref[:, kv * qw + g * gw : kv * qw + (g + 1) * gw]
            got = jnp.dot(flat, w, preferred_element_type=F32)
            got = got.reshape(pn.rows, pn.cols // OCT, OCT, gw)
            for o in range(1, pn.octets - 1):
                ext[g, pl.ds(pn.own_at(o), pn.half), kv * gw : (kv + 1) * gw] = (
                    got[:, o - 1].reshape(pn.half, gw).astype(BF16)
                )
        run(halo, below, pn.lon_ids + pn.near_ids, g, "start")

    if pn.group_all:
        slot = dp * 4 + lat
        fall[slot] = flat

        def flip(kind):
            return ((1 - dp, lat, lon), (dp, lax.rem(lat + 2, 4), lon), (dp, lat + 1 - 2 * lax.rem(lat, 2), lon))[kind]

        def slot_of(ddp, dx):
            return (dp + ddp - 2 * dp * ddp) * 4 + lax.rem(lat + 2 * dx, 4)

        hops = [(0, 0, 0), (1, 0, 0), (2, 0, 0), (1, 1, 0), (2, 1, 0), (2, 0, 1), (2, 1, 1)]

        def hop(n):
            kind, ddp, dx = hops[n]
            s = slot_of(ddp, dx)
            return remote(fall.at[s], fall.at[s], fs.at[n], fr.at[n], flip(kind))

        def hop_in(n):
            kind, ddp, dx = hops[n]
            if kind == 0:
                s = slot_of(1 - ddp, dx)
            elif kind == 1:
                s = slot_of(ddp, 1 - dx)
            else:
                mate = lat + 1 - 2 * lax.rem(lat, 2)
                s = (dp + ddp - 2 * dp * ddp) * 4 + lax.rem(mate + 2 * dx, 4)
            return remote(fall.at[s], fall.at[s], fs.at[n], fr.at[n], flip(kind))

        for n in (0, 1, 2):
            hop(n).start()

    lane = lax.broadcasted_iota(jnp.int32, (pn.nq, gw), 1)
    for g in range(pn.groups):
        got = jnp.dot(flat, wq_ref[:, g * gw : (g + 1) * gw], preferred_element_type=F32)
        dout = d_ref[:, g * gw : (g + 1) * gw].astype(F32)
        for hh in range(2):
            mine = (lane < hd) if hh == 0 else (lane >= hd)
            q2[g, hh * pn.nq : (hh + 1) * pn.nq] = jnp.where(mine, got, 0.0).astype(BF16)
            do2[g, hh * pn.nq : (hh + 1) * pn.nq] = jnp.where(mine, dout, 0.0).astype(BF16)

    nlat_all, nlon_all = valid_ref.shape

    def parts_of(n):
        shape = (pn.octets, pn.ext, OCT, n)
        o, row, c = (lax.broadcasted_iota(jnp.int32, shape, k).reshape(pn.nk, n) for k in range(3))
        return o * OCT + c, row, lax.broadcasted_iota(jnp.int32, (pn.nk, n), 1)

    col, row, li = parts_of(nlat_all)
    pick_row = jnp.where(li == row - pn.reach + lat * pn.rows, 1.0, 0.0).astype(BF16)
    col, row, li = parts_of(nlon_all)
    here = col - OCT + lon * pn.cols
    here = jnp.where(here < 0, here + nlon_all, here)
    here = jnp.where(here >= nlon_all, here - nlon_all, here)
    pick_col = li == here
    ones = jnp.ones((nlon_all, pn.nq), BF16)

    def key_values(ref):
        rows_of = jnp.dot(pick_row, ref[...].astype(F32).astype(BF16), preferred_element_type=F32)
        return jnp.dot(jnp.where(pick_col, rows_of, 0.0).astype(BF16), ones, preferred_element_type=F32)

    land = key_values(land_ref)
    ok = key_values(valid_ref)
    col, row, li = parts_of(pn.nq)
    a = row - li // pn.cols
    b = col - OCT + pn.reach - li % pn.cols
    side = 2 * pn.reach
    inside = (a >= 0) & (a <= side) & (b >= 0) & (b <= side)
    centre = (a == pn.reach) & (b == pn.reach)
    okay[...] = jnp.where(inside, jnp.where(centre, 1.0, ok), 0.0)
    per = pn.nq // pn.cols
    keys, width = pn.octets * OCT, 4 * pn.nq
    ar = lax.broadcasted_iota(jnp.int32, (16, width), 0)
    tr = lax.broadcasted_iota(jnp.int32, (16, width), 1) // pn.cols
    hot = jnp.where(ar == pn.ext - 1 - tr, 1.0, 0.0)
    spread = jnp.dot(lines_ref[...], hot, precision=lax.Precision.HIGHEST, preferred_element_type=F32)
    turn = lax.broadcasted_iota(jnp.int32, (keys, width), 1) % pn.cols
    for g in range(pn.groups):
        run(halo, above, pn.lon_ids, g, "wait_recv")
        run(halo, below, pn.corner_ids, g, "start")
        for hh in range(2):
            h = 2 * g + hh
            shifted = spread[h * keys : (h + 1) * keys]
            bit = 1
            while bit < pn.cols:
                shifted = jnp.where((turn & bit) != 0, pltpu.roll(shifted, bit, 0), shifted)
                bit *= 2
            for o in range(pn.octets):
                line = shifted[o * OCT : (o + 1) * OCT]
                for k in range(min(per, pn.ext)):
                    turned = line if k == 0 else pltpu.roll(line, width - k * pn.cols, 1)
                    for m in range((pn.ext - 1) // per + 1):
                        r = pn.ext - 1 - (m * per + k)
                        if r < 0:
                            continue
                        first = (o * pn.ext + r) * OCT
                        bias[g, first : first + OCT, hh * pn.nq : (hh + 1) * pn.nq] = (
                            turned[:, m * pn.nq : (m + 1) * pn.nq]
                            + land_bias_ref[h] * land[first : first + OCT]
                        )

    def step(g, carry):
        run(halo, above, pn.lat_ids, g, "wait_recv")
        key = ext[g, :, 0:gw]
        value = ext[g, :, gw : 2 * gw]
        qg, dg = q2[g], do2[g]
        raw = lax.dot_general(key, qg, NEAR, preferred_element_type=F32) * scale + bias[g]
        dots = lax.dot_general(value, dg, NEAR, preferred_element_type=F32)
        bent = jnp.tanh(raw * (1.0 / CAP))
        ok1 = okay[...]
        expd = jnp.exp(CAP * bent) * jnp.concatenate([ok1, ok1], axis=1)
        weight = expd * (1.0 / jnp.sum(expd, axis=0, keepdims=True))
        delta = jnp.sum(weight * dots, axis=0, keepdims=True)
        ds = (weight * (dots - delta) * ((1.0 - bent * bent) * scale)).astype(BF16)
        wb = weight.astype(BF16)
        for kv, (left, right) in enumerate(((ds, qg), (wb, dg))):
            got = jnp.dot(left, right, preferred_element_type=F32)
            for o in range(pn.octets):
                own[g, pl.ds(o * pn.half, pn.half), kv * gw : (kv + 1) * gw] = got[
                    pn.own_at(o) : pn.own_at(o) + pn.half
                ]
            gsend[g, :, kv * gw : (kv + 1) * gw] = got.astype(BF16)
        run(back, above, pn.lat_ids, g, "start")
        turned = lax.dot_general(key, ds, TALL, preferred_element_type=F32)
        both = jnp.concatenate([turned[:hd, : pn.nq], turned[hd:, pn.nq :]], axis=0)
        dq_s[g] = both.T.astype(BF16)
        return carry

    def summed(g, o, parts):
        total = own[g, pl.ds(o * pn.half, pn.half)]
        for step_, part, owner, start, count, where in pn.regions:
            if owner != o or part not in parts:
                continue
            add = grecv[g, pl.ds(where, count)].astype(F32)
            if count < pn.half:
                zero = jnp.zeros((pn.half - count, add.shape[1]), F32)
                add = jnp.concatenate([zero, add] if start else [add, zero], axis=0)
            total = total + add
        return total

    def sideways(g):
        run(back, below, pn.lat_ids, g, "wait_recv")
        for o in (0, pn.octets - 1):
            gsend[g, pl.ds(pn.own_at(o), pn.half)] = summed(g, o, (-1, 1)).astype(BF16)
        run(back, below, pn.lon_ids, g, "start")

    def later(g, carry):
        step(g, carry)
        sideways(g - 1)
        return carry

    if pn.group_all:
        step(0, 0)
        hop_in(0).wait_recv()
        hop(3).start()
        hop(4).start()
        lax.fori_loop(1, pn.groups - 1, later, 0)
        hop_in(1).wait_recv()
        hop(5).start()
        hop_in(3).wait_recv()
        hop(6).start()
        lax.fori_loop(pn.groups - 1, pn.groups, later, 0)
    else:
        step(0, 0)
        lax.fori_loop(1, pn.groups, later, 0)

    dq = jnp.concatenate([dq_s[g] for g in range(pn.groups)], axis=1)
    first = lax.dot_general(dq, wq_ref[...], NEAR, preferred_element_type=F32)
    sideways(pn.groups - 1)
    if pn.group_all:
        fsum[...] = first

        def kcopy(n, out):
            d, x = n // 4, n % 4
            tdp = lax.rem(dp + d, 2)
            tlat = lax.rem(lat + x, 4)
            fdp = lax.rem(dp + d, 2)
            flat_ = lax.rem(lat + 4 - x, 4)
            to = tdp * 4 + tlat
            frm = slot if out else fdp * 4 + flat_
            return remote(
                cell.at[to], kall.at[frm], ks.at[n], kr.at[n], (tdp, tlat, lon)
            )

        target = cell
    pieces = {}
    for g in range(pn.groups):
        run(back, below, pn.lon_ids, g, "wait_recv")
        halves = []
        for o in range(1, pn.octets - 1):
            total = summed(g, o, (-1, 0, 1))
            halves.append(total.reshape(pn.rows, 1, OCT, 2 * gw))
        full = jnp.concatenate(halves, axis=1).reshape(pn.nq, 2 * gw).astype(BF16)
        for kv in range(2):
            pieces[kv * pn.groups + g] = full[:, kv * gw : (kv + 1) * gw]
            if pn.group_all:
                cell[kv * pn.groups + g] = full[:, kv * gw : (kv + 1) * gw]
    if pn.group_all:
        for n in range(1, 8):
            kcopy(n, True).start()
    cells = jnp.concatenate([pieces[k] for k in range(2 * pn.groups)], axis=1)
    second = lax.dot_general(cells, wkv_ref[...], NEAR, preferred_element_type=F32)
    if not pn.group_all:
        cell_out[...] = cells
        fg_out[...] = (first + second).astype(BF16)
    else:
        fg_out[...] = (fsum[...] + second).astype(BF16)
        kall[slot] = cell[slot]
        for n in (2, 4, 5, 6):
            hop_in(n).wait_recv()
        for n in range(1, 8):
            kcopy(n, False).wait_recv()
        ka = kall[...].reshape(8 * pn.nq, gw)
        fa = fall[...].reshape(8 * pn.nq, fall.shape[2])
        grad = lax.dot_general(ka, fa, TALL, preferred_element_type=F32).T
        depth = grad.shape[0] // (8 * nlon)
        grad = (grad * norm).reshape(8, nlon, depth, gw)

        def zcopy(n):
            to = lax.rem(lon + n, nlon)
            return remote(zsend.at[to], zrecv.at[n - 1], zs.at[n - 1], zr.at[n - 1], (dp, lat, to))

        for z in range(nlon):
            zsend[z] = grad[:, z].reshape(8 * depth, gw).astype(BF16)
        for n in range(1, nlon):
            zcopy(n).start()
        for n in range(1, nlon):
            zcopy(n).wait_recv()
        total = zsend[lon].astype(F32)
        for n in range(1, nlon):
            total = total + zrecv[n - 1].astype(F32)
        ocol[...] = total.reshape(8, depth, gw)

        def ocopy(n, out):
            d, x = n // 4, n % 4
            tdp = lax.rem(dp + d, 2)
            tlat = lax.rem(lat + x, 4)
            frm = slot if out else tdp * 4 + lax.rem(lat + 4 - x, 4)
            where = pl.ds(pl.multiple_of(frm * gw, gw), gw)
            return remote(
                ocol.at[tdp * 4 + tlat], kv_out.at[:, where], os_.at[n], or_.at[n], (tdp, tlat, lon)
            )

        for n in range(1, 8):
            ocopy(n, True).start()
        kv_out[:, pl.ds(pl.multiple_of(slot * gw, gw), gw)] = ocol[slot]
        for n in range(1, 8):
            ocopy(n, False).wait_recv()
        for n in range(1, 8):
            kcopy(n, True).wait_send()
            ocopy(n, True).wait_send()
        for n in range(1, nlon):
            zcopy(n).wait_send()
        for n in range(7):
            hop(n).wait_send()
    for g in range(pn.groups):
        run(halo, below, pn.lon_ids + pn.lat_ids, g, "wait_send")
        run(back, above, pn.lat_ids, g, "wait_send")
        run(back, above, pn.lon_ids, g, "wait_send")


def padded_bias(position_bias, pn):
    heads, side, _ = position_bias.shape
    lead, keys = OCT - pn.reach, pn.octets * OCT
    turned = jnp.swapaxes(position_bias, 1, 2)
    turned = jnp.pad(turned, ((0, 0), (lead, keys - side - lead), (0, 16 - side)))
    return turned.reshape(heads * keys, 16)


def shards(
    fields, cotangent, query_weight, keyval_weight, position_bias, land_bias, valid_cell, land_sea
):
    rows, cols, width = fields.shape[1:]
    q_width = query_weight.shape[1]
    heads = position_bias.shape[0]
    size = q_width // heads
    reach = (position_bias.shape[1] - 1) // 2
    nlat, nlon, ndp = lax.axis_size("lat"), lax.axis_size("lon"), lax.axis_size("dp")
    pn = Plan(rows, cols, reach, heads, size, nlat, nlon, ndp)
    flat = fields.reshape(pn.nq, width)
    dout = cotangent.reshape(pn.nq, q_width)
    devices = nlat * nlon * ndp
    norm = float(pn.nq * devices) ** (-0.5)
    gw = 2 * size
    vm = pl.BlockSpec(memory_space=pltpu.VMEM)
    dma = pltpu.SemaphoreType.DMA
    nreg = len(pn.regions)
    g = pn.groups
    scratch = [
        pltpu.VMEM((g, pn.nk, 2 * gw), BF16),
        pltpu.VMEM((g, pn.nk, 2 * gw), BF16),
        pltpu.VMEM((g, pn.nk, 2 * gw), BF16),
        pltpu.VMEM((g, pn.octets * pn.half, 2 * gw), F32),
        pltpu.VMEM((g, 2 * pn.nq, gw), BF16),
        pltpu.VMEM((g, 2 * pn.nq, gw), BF16),
        pltpu.VMEM((g, pn.nk, 2 * pn.nq), F32),
        pltpu.VMEM((pn.nk, pn.nq), F32),
        pltpu.VMEM((g, pn.nq, gw), BF16),
        dma((g, nreg)), dma((g, nreg)), dma((g, nreg)), dma((g, nreg)),
    ]
    out_shape = [jax.ShapeDtypeStruct((pn.nq, width), BF16)]
    if pn.group_all:
        depth = width // devices
        out_shape.append(jax.ShapeDtypeStruct((depth, 2 * q_width), F32))
        scratch += [
            pltpu.VMEM((8, pn.nq, width), BF16),
            pltpu.VMEM((8, pn.nq, gw), BF16),
            pltpu.VMEM((8, pn.nq, gw), BF16),
            pltpu.VMEM((nlon, 8 * depth, gw), BF16),
            pltpu.VMEM((nlon - 1, 8 * depth, gw), BF16),
            pltpu.VMEM((pn.nq, width), F32),
            pltpu.VMEM((8, depth, gw), F32),
            dma((7,)), dma((7,)), dma((8,)), dma((8,)),
            dma((nlon - 1,)), dma((nlon - 1,)), dma((8,)), dma((8,)),
        ]
    else:
        out_shape.append(jax.ShapeDtypeStruct((pn.nq, 2 * q_width), BF16))

    def kernel(*refs):
        body(pn, size ** (-0.5), norm, refs)

    field_grad, other = pl.pallas_call(
        kernel,
        out_shape=out_shape,
        in_specs=[vm] * 5 + [pl.BlockSpec(memory_space=pltpu.SMEM)] + [vm] * 2,
        out_specs=[vm, vm],
        scratch_shapes=scratch,
        name="attention_grads",
        compiler_params=pltpu.CompilerParams(
            collective_id=0, has_side_effects=True, vmem_limit_bytes=48 * 1024 * 1024
        ),
    )(
        flat, dout, query_weight, keyval_weight, padded_bias(position_bias, pn), land_bias,
        valid_cell, land_sea,
    )
    field_grad = field_grad.reshape(1, rows, cols, width)
    if pn.group_all:
        return field_grad, other
    term = lax.dot_general(flat, other, (((0,), (0,)), ((), ())), preferred_element_type=F32)
    keyval_grad = lax.psum_scatter(
        term * norm, ("dp", "lat", "lon"), scatter_dimension=0, tiled=True
    )
    return field_grad, keyval_grad


def solution(mesh):
    block = P("dp", "lat", "lon", None)
    in_specs = (block, block, P(), P(), P(), P(), P(), P())
    out_specs = (block, P(("dp", "lat", "lon"), None))
    return jax.shard_map(shards, mesh=mesh, in_specs=in_specs, out_specs=out_specs, check_vma=False)
```

```python
import jax
import jax.numpy as jnp
from jax import lax
from jax.experimental import pallas as pl
from jax.experimental.pallas import tpu as pltpu
from jax.sharding import PartitionSpec as P

CAP = 20.0
MESH = pl.DeviceIdType.MESH
F32, BF16 = jnp.float32, jnp.bfloat16
OCT = 8
NEAR = (((1,), (1,)), ((), ()))
TALL = (((0,), (0,)), ((), ()))


class Plan:
    def __init__(self, rows, cols, reach, heads, size, lat, lon, dp):
        self.rows, self.cols, self.reach, self.heads, self.size = rows, cols, reach, heads, size
        self.lat, self.lon, self.dp = lat, lon, dp
        self.nq = rows * cols
        self.ext = rows + 2 * reach
        self.octets = cols // OCT + 2
        self.per_oct = self.ext * OCT
        self.nk = self.octets * self.per_oct
        self.half = rows * OCT
        self.groups = heads // 2
        self.edge = reach * OCT
        self.regions = []
        last = self.octets - 1
        for o in range(self.octets):
            for part in (-1, 0, 1):
                step = (-1 if o == 0 else (1 if o == last else 0)) if part == 0 else 0
                if step == 0 and part == 0:
                    continue
                owner = (last - 1 if o == 0 else 1) if part == 0 else o
                start = (self.half - self.edge) if part == -1 else 0
                count = self.half if part == 0 else self.edge
                at = o * self.per_oct + (0 if part == -1 else self.edge + (0 if part == 0 else self.half))
                self.regions.append((step, part, owner, start, count, at))
        self.lon_ids = [i for i, r in enumerate(self.regions) if r[1] == 0]
        self.near_ids = [i for i, r in enumerate(self.regions) if r[1] and 0 < r[2] < last]
        self.corner_ids = [i for i, r in enumerate(self.regions) if r[1] and r[2] in (0, last)]
        self.lat_ids = self.near_ids + self.corner_ids
        self.group_all = dp == 2 and lat == 4 and self.groups == 4

    def own_at(self, o):
        return o * self.per_oct + self.edge


def body(pn, scale, norm, refs):
    (f_hbm, d_hbm, wq_hbm, wkv_hbm, lines_ref, land_bias_ref, valid_hbm, land_hbm) = refs[:8]
    if pn.group_all:
        fg_out, kv_out = refs[8:10]
        rest = refs[10:]
    else:
        fg_out, cell_out = refs[8:10]
        rest = refs[10:]
    (ext, gsend, grecv, own, q2, do2, bias, okay, dq_s, hs, hr, gs, gr) = rest[:13]
    (f_ref, d_ref, wq_ref, wkv_ref, valid_ref, land_ref, cell, ins) = rest[13:21]
    if pn.group_all:
        (fall, kall, zsend, zrecv, fsum, ocol, fs, fr, ks, kr, zs, zr, os_, or_) = rest[21:]
    lat, lon, dp = lax.axis_index("lat"), lax.axis_index("lon"), lax.axis_index("dp")
    nlat, nlon = pn.lat, pn.lon
    hd = pn.size
    gw = 2 * hd
    qw = pn.heads * hd

    def at(dlat, dlon, ddp=0):
        return (
            lax.rem(dp + ddp, pn.dp) if ddp else dp,
            lax.rem(lat + dlat + nlat, nlat) if dlat else lat,
            lax.rem(lon + dlon + nlon, nlon) if dlon else lon,
        )

    peers = [(0, a, b) for a in (-1, 0, 1) for b in (-1, 0, 1) if (a == 0) != (b == 0)]
    if pn.group_all:
        steps = [(d, a, 0) for d in range(2) for a in range(-1, 3) if d or a]
        steps += [(0, 0, b) for b in range(1, nlon)]
        for d, a, b in steps:
            seen = {(u, v % nlat, w % nlon) for u, v, w in peers}
            if (d, a % nlat, b % nlon) not in seen:
                peers.append((d, a, b))
    def bring(n):
        if n < 2 * pn.groups:
            part = pl.ds(((n % 2) * pn.groups + n // 2) * gw, gw)
            src, dst = wkv_hbm.at[:, part], wkv_ref.at[:, part]
        else:
            src, dst = (
                (f_hbm, f_ref), (wq_hbm, wq_ref), (d_hbm, d_ref), (valid_hbm, valid_ref), (land_hbm, land_ref)
            )[n - 2 * pn.groups]
        return pltpu.make_async_copy(src, dst, ins.at[n])

    last_in = 2 * pn.groups
    bring(last_in).start()
    for n in range(last_in):
        bring(n).start()
    for n in range(last_in + 1, last_in + 5):
        bring(n).start()
    barrier = pltpu.get_barrier_semaphore()
    for d, a, b in peers:
        pl.semaphore_signal(barrier, inc=1, device_id=at(a, b, d), device_id_type=MESH)
    pl.semaphore_wait(barrier, len(peers))

    def remote(src, dst, ssem, rsem, dev):
        return pltpu.make_async_remote_copy(
            src_ref=src, dst_ref=dst, send_sem=ssem, recv_sem=rsem, device_id=dev, device_id_type=MESH
        )

    def halo(g, i):
        step, part, owner, start, count, where = pn.regions[i]
        return remote(
            ext.at[g, pl.ds(pn.own_at(owner) + start, count)],
            ext.at[g, pl.ds(where, count)],
            hs.at[g, i], hr.at[g, i], at(-part, -step),
        )

    def back(g, i):
        step, part, owner, start, count, where = pn.regions[i]
        return remote(
            gsend.at[g, pl.ds(where, count)],
            grecv.at[g, pl.ds(where, count)],
            gs.at[g, i], gr.at[g, i], at(part, step),
        )

    def only(cond, act):
        if cond is None:
            act()
        else:
            pl.when(cond)(act)

    def below(part):
        return None if part == 0 else (lat < nlat - 1 if part == -1 else lat > 0)

    def above(part):
        return below(-part)

    def run(make, side, ids, g, what):
        for part in (-1, 0, 1):
            chosen = [i for i in ids if pn.regions[i][1] == part]
            if chosen:
                only(side(part), lambda: [getattr(make(g, i), what)() for i in chosen] and None)

    for part in (-1, 1):
        def clear(part=part):
            for g in range(pn.groups):
                for step, p, owner, start, count, where in pn.regions:
                    if p == part:
                        ext[g, pl.ds(where, count)] = jnp.zeros((count, 2 * gw), BF16)
                    if p == -part:
                        grecv[g, pl.ds(where, count)] = jnp.zeros((count, 2 * gw), BF16)

        pl.when(lat == (0 if part == -1 else nlat - 1))(clear)

    bring(last_in).wait()
    flat = f_ref[...]
    for g in range(pn.groups):
        bring(2 * g).wait()
        bring(2 * g + 1).wait()
        for kv in range(2):
            w = wkv_ref[:, kv * qw + g * gw : kv * qw + (g + 1) * gw]
            got = jnp.dot(flat, w, preferred_element_type=F32)
            got = got.reshape(pn.rows, pn.cols // OCT, OCT, gw)
            for o in range(1, pn.octets - 1):
                ext[g, pl.ds(pn.own_at(o), pn.half), kv * gw : (kv + 1) * gw] = (
                    got[:, o - 1].reshape(pn.half, gw).astype(BF16)
                )
        run(halo, below, pn.lon_ids + pn.near_ids, g, "start")

    if pn.group_all:
        slot = dp * 4 + lat
        fall[slot] = flat

        def flip(kind):
            return ((1 - dp, lat, lon), (dp, lax.rem(lat + 2, 4), lon), (dp, lat + 1 - 2 * lax.rem(lat, 2), lon))[kind]

        def slot_of(ddp, dx):
            return (dp + ddp - 2 * dp * ddp) * 4 + lax.rem(lat + 2 * dx, 4)

        hops = [(0, 0, 0), (1, 0, 0), (2, 0, 0), (1, 1, 0), (2, 1, 0), (2, 0, 1), (2, 1, 1)]

        def hop(n):
            kind, ddp, dx = hops[n]
            s = slot_of(ddp, dx)
            return remote(fall.at[s], fall.at[s], fs.at[n], fr.at[n], flip(kind))

        def hop_in(n):
            kind, ddp, dx = hops[n]
            if kind == 0:
                s = slot_of(1 - ddp, dx)
            elif kind == 1:
                s = slot_of(ddp, 1 - dx)
            else:
                mate = lat + 1 - 2 * lax.rem(lat, 2)
                s = (dp + ddp - 2 * dp * ddp) * 4 + lax.rem(mate + 2 * dx, 4)
            return remote(fall.at[s], fall.at[s], fs.at[n], fr.at[n], flip(kind))

        for n in (0, 2):
            hop(n).start()
    for n in range(last_in + 1, last_in + 5):
        bring(n).wait()

    lane = lax.broadcasted_iota(jnp.int32, (pn.nq, gw), 1)
    for g in range(pn.groups):
        got = jnp.dot(flat, wq_ref[:, g * gw : (g + 1) * gw], preferred_element_type=F32)
        dout = d_ref[:, g * gw : (g + 1) * gw].astype(F32)
        for hh in range(2):
            mine = (lane < hd) if hh == 0 else (lane >= hd)
            q2[g, hh * pn.nq : (hh + 1) * pn.nq] = jnp.where(mine, got, 0.0).astype(BF16)
            do2[g, hh * pn.nq : (hh + 1) * pn.nq] = jnp.where(mine, dout, 0.0).astype(BF16)

    nlat_all, nlon_all = valid_ref.shape

    def parts_of(n):
        shape = (pn.octets, pn.ext, OCT, n)
        o, row, c = (lax.broadcasted_iota(jnp.int32, shape, k).reshape(pn.nk, n) for k in range(3))
        return o * OCT + c, row, lax.broadcasted_iota(jnp.int32, (pn.nk, n), 1)

    col, row, li = parts_of(nlat_all)
    pick_row = jnp.where(li == row - pn.reach + lat * pn.rows, 1.0, 0.0).astype(BF16)
    col, row, li = parts_of(nlon_all)
    here = col - OCT + lon * pn.cols
    here = jnp.where(here < 0, here + nlon_all, here)
    here = jnp.where(here >= nlon_all, here - nlon_all, here)
    pick_col = li == here
    ones = jnp.ones((nlon_all, pn.nq), BF16)

    def key_values(ref):
        rows_of = jnp.dot(pick_row, ref[...].astype(F32).astype(BF16), preferred_element_type=F32)
        return jnp.dot(jnp.where(pick_col, rows_of, 0.0).astype(BF16), ones, preferred_element_type=F32)

    land = key_values(land_ref)
    ok = key_values(valid_ref)
    col, row, li = parts_of(pn.nq)
    a = row - li // pn.cols
    b = col - OCT + pn.reach - li % pn.cols
    side = 2 * pn.reach
    inside = (a >= 0) & (a <= side) & (b >= 0) & (b <= side)
    centre = (a == pn.reach) & (b == pn.reach)
    okay[...] = jnp.where(inside, jnp.where(centre, 1.0, ok), 0.0)
    per = pn.nq // pn.cols
    keys, width = pn.octets * OCT, 4 * pn.nq
    ar = lax.broadcasted_iota(jnp.int32, (16, width), 0)
    tr = lax.broadcasted_iota(jnp.int32, (16, width), 1) // pn.cols
    hot = jnp.where(ar == pn.ext - 1 - tr, 1.0, 0.0)
    spread = jnp.dot(lines_ref[...], hot, precision=lax.Precision.HIGHEST, preferred_element_type=F32)
    turn = lax.broadcasted_iota(jnp.int32, (keys, width), 1) % pn.cols
    for g in range(pn.groups):
        run(halo, above, pn.lon_ids, g, "wait_recv")
        run(halo, below, pn.corner_ids, g, "start")
        for hh in range(2):
            h = 2 * g + hh
            shifted = spread[h * keys : (h + 1) * keys]
            bit = 1
            while bit < pn.cols:
                shifted = jnp.where((turn & bit) != 0, pltpu.roll(shifted, bit, 0), shifted)
                bit *= 2
            for o in range(pn.octets):
                line = shifted[o * OCT : (o + 1) * OCT]
                for k in range(min(per, pn.ext)):
                    turned = line if k == 0 else pltpu.roll(line, width - k * pn.cols, 1)
                    for m in range((pn.ext - 1) // per + 1):
                        r = pn.ext - 1 - (m * per + k)
                        if r < 0:
                            continue
                        first = (o * pn.ext + r) * OCT
                        bias[g, first : first + OCT, hh * pn.nq : (hh + 1) * pn.nq] = (
                            turned[:, m * pn.nq : (m + 1) * pn.nq]
                            + land_bias_ref[h] * land[first : first + OCT]
                        )

    def step(g, carry):
        run(halo, above, pn.lat_ids, g, "wait_recv")
        key = ext[g, :, 0:gw]
        value = ext[g, :, gw : 2 * gw]
        qg, dg = q2[g], do2[g]
        raw = lax.dot_general(key, qg, NEAR, preferred_element_type=F32) * scale + bias[g]
        dots = lax.dot_general(value, dg, NEAR, preferred_element_type=F32)
        bent = jnp.tanh(raw * (1.0 / CAP))
        ok1 = okay[...]
        expd = jnp.exp(CAP * bent) * jnp.concatenate([ok1, ok1], axis=1)
        weight = expd * (1.0 / jnp.sum(expd, axis=0, keepdims=True))
        delta = jnp.sum(weight * dots, axis=0, keepdims=True)
        ds = (weight * (dots - delta) * ((1.0 - bent * bent) * scale)).astype(BF16)
        wb = weight.astype(BF16)
        for kv, (left, right) in enumerate(((ds, qg), (wb, dg))):
            got = jnp.dot(left, right, preferred_element_type=F32)
            for o in range(pn.octets):
                own[g, pl.ds(o * pn.half, pn.half), kv * gw : (kv + 1) * gw] = got[
                    pn.own_at(o) : pn.own_at(o) + pn.half
                ]
            gsend[g, :, kv * gw : (kv + 1) * gw] = got.astype(BF16)
        run(back, above, pn.lat_ids, g, "start")
        turned = lax.dot_general(key, ds, TALL, preferred_element_type=F32)
        both = jnp.concatenate([turned[:hd, : pn.nq], turned[hd:, pn.nq :]], axis=0)
        dq_s[g] = both.T.astype(BF16)
        return carry

    def summed(g, o, parts):
        total = own[g, pl.ds(o * pn.half, pn.half)]
        for step_, part, owner, start, count, where in pn.regions:
            if owner != o or part not in parts:
                continue
            add = grecv[g, pl.ds(where, count)].astype(F32)
            if count < pn.half:
                zero = jnp.zeros((pn.half - count, add.shape[1]), F32)
                add = jnp.concatenate([zero, add] if start else [add, zero], axis=0)
            total = total + add
        return total

    def sideways(g):
        run(back, below, pn.lat_ids, g, "wait_recv")
        for o in (0, pn.octets - 1):
            gsend[g, pl.ds(pn.own_at(o), pn.half)] = summed(g, o, (-1, 1)).astype(BF16)
        run(back, below, pn.lon_ids, g, "start")

    def kcopy(g, kv):
        to = kv * pn.groups + g
        return remote(cell.at[to], kall.at[slot], ks.at[to], kr.at[slot], (kv, g, lon))

    def kcopy_in(n):
        frm = lax.rem(slot + n, 8)
        return remote(cell.at[frm], kall.at[frm], ks.at[frm], kr.at[frm], (frm // 4, lax.rem(frm, 4), lon))

    def finish(g):
        run(back, below, pn.lon_ids, g, "wait_recv")
        halves = []
        for o in range(1, pn.octets - 1):
            halves.append(summed(g, o, (-1, 0, 1)).reshape(pn.rows, 1, OCT, 2 * gw))
        full = jnp.concatenate(halves, axis=1).reshape(pn.nq, 2 * gw).astype(BF16)
        for kv in range(2):
            cell[kv * pn.groups + g] = full[:, kv * gw : (kv + 1) * gw]
            if pn.group_all:
                pl.when(kv * pn.groups + g != slot)(lambda kv=kv: kcopy(g, kv).start())

    def later(g, carry):
        step(g, carry)
        sideways(g - 1)
        return carry

    def last(g, carry):
        later(g, carry)
        finish(g - 2)
        return carry

    if pn.group_all:
        step(0, 0)
        hop_in(0).wait_recv()
        for n in (1, 3, 4):
            hop(n).start()
    else:
        step(0, 0)
    later(1, 0)
    lax.fori_loop(2, pn.groups, last, 0)
    sideways(pn.groups - 1)
    finish(pn.groups - 2)

    dq = jnp.concatenate([dq_s[g] for g in range(pn.groups)], axis=1)
    first = lax.dot_general(dq, wq_ref[...], NEAR, preferred_element_type=F32)
    if pn.group_all:
        fsum[...] = first
        hop_in(1).wait_recv()
        hop(5).start()
        hop_in(3).wait_recv()
        hop(6).start()
    finish(pn.groups - 1)
    cells = jnp.concatenate([cell[k] for k in range(2 * pn.groups)], axis=1)
    second = lax.dot_general(cells, wkv_ref[...], NEAR, preferred_element_type=F32)
    if not pn.group_all:
        cell_out[...] = cells
        fg_out[...] = (first + second).astype(BF16)
    else:
        fg_out[...] = (fsum[...] + second).astype(BF16)
        kall[slot] = cell[slot]
        for n in (2, 4, 5, 6):
            hop_in(n).wait_recv()
        for n in range(1, 8):
            kcopy_in(n).wait_recv()
        ka = kall[...].reshape(8 * pn.nq, gw)
        fa = fall[...].reshape(8 * pn.nq, fall.shape[2])
        grad = lax.dot_general(ka, fa, TALL, preferred_element_type=F32).T
        depth = grad.shape[0] // (8 * nlon)
        grad = (grad * norm).reshape(8, nlon, depth, gw)

        def zcopy(n):
            to = lax.rem(lon + n, nlon)
            return remote(zsend.at[to], zrecv.at[n - 1], zs.at[n - 1], zr.at[n - 1], (dp, lat, to))

        for z in range(nlon):
            zsend[z] = grad[:, z].reshape(8 * depth, gw).astype(BF16)
        for n in range(1, nlon):
            zcopy(n).start()
        for n in range(1, nlon):
            zcopy(n).wait_recv()
        total = zsend[lon].astype(F32)
        for n in range(1, nlon):
            total = total + zrecv[n - 1].astype(F32)
        ocol[...] = total.reshape(8, depth, gw)

        def ocopy(n, out):
            d, x = n // 4, n % 4
            tdp = lax.rem(dp + d, 2)
            tlat = lax.rem(lat + x, 4)
            frm = slot if out else tdp * 4 + lax.rem(lat + 4 - x, 4)
            where = pl.ds(pl.multiple_of(frm * gw, gw), gw)
            return remote(
                ocol.at[tdp * 4 + tlat], kv_out.at[:, where], os_.at[n], or_.at[n], (tdp, tlat, lon)
            )

        for n in range(1, 8):
            ocopy(n, True).start()
        kv_out[:, pl.ds(pl.multiple_of(slot * gw, gw), gw)] = ocol[slot]
        for n in range(1, 8):
            ocopy(n, False).wait_recv()
        for n in range(1, 8):
            kcopy_in(n).wait_send()
            ocopy(n, True).wait_send()
        for n in range(1, nlon):
            zcopy(n).wait_send()
        for n in range(7):
            hop(n).wait_send()
    for g in range(pn.groups):
        run(halo, below, pn.lon_ids + pn.lat_ids, g, "wait_send")
        run(back, above, pn.lat_ids, g, "wait_send")
        run(back, above, pn.lon_ids, g, "wait_send")


def padded_bias(position_bias, pn):
    heads, side, _ = position_bias.shape
    lead, keys = OCT - pn.reach, pn.octets * OCT
    turned = jnp.swapaxes(position_bias, 1, 2)
    turned = jnp.pad(turned, ((0, 0), (lead, keys - side - lead), (0, 16 - side)))
    return turned.reshape(heads * keys, 16)


def shards(
    fields, cotangent, query_weight, keyval_weight, position_bias, land_bias, valid_cell, land_sea
):
    rows, cols, width = fields.shape[1:]
    q_width = query_weight.shape[1]
    heads = position_bias.shape[0]
    size = q_width // heads
    reach = (position_bias.shape[1] - 1) // 2
    nlat, nlon, ndp = lax.axis_size("lat"), lax.axis_size("lon"), lax.axis_size("dp")
    pn = Plan(rows, cols, reach, heads, size, nlat, nlon, ndp)
    flat = fields.reshape(pn.nq, width)
    dout = cotangent.reshape(pn.nq, q_width)
    devices = nlat * nlon * ndp
    norm = float(pn.nq * devices) ** (-0.5)
    gw = 2 * size
    vm = pl.BlockSpec(memory_space=pltpu.VMEM)
    hbm = pl.BlockSpec(memory_space=pl.ANY)
    dma = pltpu.SemaphoreType.DMA
    nreg = len(pn.regions)
    g = pn.groups
    scratch = [
        pltpu.VMEM((g, pn.nk, 2 * gw), BF16),
        pltpu.VMEM((g, pn.nk, 2 * gw), BF16),
        pltpu.VMEM((g, pn.nk, 2 * gw), BF16),
        pltpu.VMEM((g, pn.octets * pn.half, 2 * gw), F32),
        pltpu.VMEM((g, 2 * pn.nq, gw), BF16),
        pltpu.VMEM((g, 2 * pn.nq, gw), BF16),
        pltpu.VMEM((g, pn.nk, 2 * pn.nq), F32),
        pltpu.VMEM((pn.nk, pn.nq), F32),
        pltpu.VMEM((g, pn.nq, gw), BF16),
        dma((g, nreg)), dma((g, nreg)), dma((g, nreg)), dma((g, nreg)),
        pltpu.VMEM((pn.nq, width), BF16),
        pltpu.VMEM((pn.nq, q_width), BF16),
        pltpu.VMEM(query_weight.shape, BF16),
        pltpu.VMEM(keyval_weight.shape, BF16),
        pltpu.VMEM(valid_cell.shape, jnp.int32),
        pltpu.VMEM(land_sea.shape, jnp.int32),
        pltpu.VMEM((2 * g, pn.nq, gw), BF16),
        dma((2 * g + 5,)),
    ]
    out_shape = [jax.ShapeDtypeStruct((pn.nq, width), BF16)]
    if pn.group_all:
        depth = width // devices
        out_shape.append(jax.ShapeDtypeStruct((depth, 2 * q_width), F32))
        scratch += [
            pltpu.VMEM((8, pn.nq, width), BF16),
            pltpu.VMEM((8, pn.nq, gw), BF16),
            pltpu.VMEM((nlon, 8 * depth, gw), BF16),
            pltpu.VMEM((nlon - 1, 8 * depth, gw), BF16),
            pltpu.VMEM((pn.nq, width), F32),
            pltpu.VMEM((8, depth, gw), F32),
            dma((7,)), dma((7,)), dma((8,)), dma((8,)),
            dma((nlon - 1,)), dma((nlon - 1,)), dma((8,)), dma((8,)),
        ]
    else:
        out_shape.append(jax.ShapeDtypeStruct((pn.nq, 2 * q_width), BF16))

    def kernel(*refs):
        body(pn, size ** (-0.5), norm, refs)

    field_grad, other = pl.pallas_call(
        kernel,
        out_shape=out_shape,
        in_specs=[hbm] * 4 + [vm, pl.BlockSpec(memory_space=pltpu.SMEM)] + [hbm] * 2,
        out_specs=[vm, vm],
        scratch_shapes=scratch,
        name="attention_grads",
        compiler_params=pltpu.CompilerParams(
            collective_id=0, has_side_effects=True, vmem_limit_bytes=60 * 1024 * 1024
        ),
    )(
        flat, dout, query_weight, keyval_weight, padded_bias(position_bias, pn), land_bias,
        valid_cell, land_sea,
    )
    field_grad = field_grad.reshape(1, rows, cols, width)
    if pn.group_all:
        return field_grad, other
    term = lax.dot_general(flat, other, (((0,), (0,)), ((), ())), preferred_element_type=F32)
    keyval_grad = lax.psum_scatter(
        term * norm, ("dp", "lat", "lon"), scatter_dimension=0, tiled=True
    )
    return field_grad, keyval_grad


def solution(mesh):
    block = P("dp", "lat", "lon", None)
    in_specs = (block, block, P(), P(), P(), P(), P(), P())
    out_specs = (block, P(("dp", "lat", "lon"), None))
    return jax.shard_map(shards, mesh=mesh, in_specs=in_specs, out_specs=out_specs, check_vma=False)
```

```python
import jax
import jax.numpy as jnp
from jax import lax
from jax.experimental import pallas as pl
from jax.experimental.pallas import tpu as pltpu
from jax.sharding import PartitionSpec as P

CAP = 20.0
MESH = pl.DeviceIdType.MESH
F32, BF16 = jnp.float32, jnp.bfloat16
OCT = 8
NEAR = (((1,), (1,)), ((), ()))
TALL = (((0,), (0,)), ((), ()))


class Plan:
    def __init__(self, rows, cols, reach, heads, size, lat, lon, dp):
        self.rows, self.cols, self.reach, self.heads, self.size = rows, cols, reach, heads, size
        self.lat, self.lon, self.dp = lat, lon, dp
        self.nq = rows * cols
        self.ext = rows + 2 * reach
        self.octets = cols // OCT + 2
        self.per_oct = self.ext * OCT
        self.nk = self.octets * self.per_oct
        self.half = rows * OCT
        self.groups = heads // 2
        self.edge = reach * OCT
        self.regions = []
        last = self.octets - 1
        for o in range(self.octets):
            for part in (-1, 0, 1):
                step = (-1 if o == 0 else (1 if o == last else 0)) if part == 0 else 0
                if step == 0 and part == 0:
                    continue
                owner = (last - 1 if o == 0 else 1) if part == 0 else o
                start = (self.half - self.edge) if part == -1 else 0
                count = self.half if part == 0 else self.edge
                at = o * self.per_oct + (0 if part == -1 else self.edge + (0 if part == 0 else self.half))
                self.regions.append((step, part, owner, start, count, at))
        self.lon_ids = [i for i, r in enumerate(self.regions) if r[1] == 0]
        self.near_ids = [i for i, r in enumerate(self.regions) if r[1] and 0 < r[2] < last]
        self.corner_ids = [i for i, r in enumerate(self.regions) if r[1] and r[2] in (0, last)]
        self.lat_ids = self.near_ids + self.corner_ids
        self.group_all = dp == 2 and lat == 4 and self.groups == 4

    def own_at(self, o):
        return o * self.per_oct + self.edge


def body(pn, scale, norm, refs):
    (f_hbm, d_hbm, wq_hbm, wkv_hbm, lines_ref, land_bias_ref, valid_hbm, land_hbm) = refs[:8]
    if pn.group_all:
        fg_out, kv_out = refs[8:10]
        rest = refs[10:]
    else:
        fg_out, cell_out = refs[8:10]
        rest = refs[10:]
    (ext, gsend, grecv, own, q2, do2, bias, okay, dq_s, hs, hr, gs, gr) = rest[:13]
    (f_ref, d_ref, wq_ref, wkv_ref, valid_ref, land_ref, cell, ins) = rest[13:21]
    if pn.group_all:
        (fall, kall, zsend, zrecv, fsum, ocol, fs, fr, ks, kr, zs, zr, os_, or_) = rest[21:]
    lat, lon, dp = lax.axis_index("lat"), lax.axis_index("lon"), lax.axis_index("dp")
    nlat, nlon = pn.lat, pn.lon
    hd = pn.size
    gw = 2 * hd
    qw = pn.heads * hd

    def at(dlat, dlon, ddp=0):
        return (
            lax.rem(dp + ddp, pn.dp) if ddp else dp,
            lax.rem(lat + dlat + nlat, nlat) if dlat else lat,
            lax.rem(lon + dlon + nlon, nlon) if dlon else lon,
        )

    peers = [(0, a, b) for a in (-1, 0, 1) for b in (-1, 0, 1) if (a == 0) != (b == 0)]
    if pn.group_all:
        steps = [(d, a, 0) for d in range(2) for a in range(-1, 3) if d or a]
        steps += [(0, 0, b) for b in range(1, nlon)]
        for d, a, b in steps:
            seen = {(u, v % nlat, w % nlon) for u, v, w in peers}
            if (d, a % nlat, b % nlon) not in seen:
                peers.append((d, a, b))
    def bring(n):
        if n < 2 * pn.groups:
            part = pl.ds(((n % 2) * pn.groups + n // 2) * gw, gw)
            src, dst = wkv_hbm.at[:, part], wkv_ref.at[:, part]
        else:
            src, dst = (
                (f_hbm, f_ref), (wq_hbm, wq_ref), (d_hbm, d_ref), (valid_hbm, valid_ref), (land_hbm, land_ref)
            )[n - 2 * pn.groups]
        return pltpu.make_async_copy(src, dst, ins.at[n])

    last_in = 2 * pn.groups
    bring(last_in).start()
    for n in range(last_in):
        bring(n).start()
    for n in range(last_in + 1, last_in + 5):
        bring(n).start()
    barrier = pltpu.get_barrier_semaphore()
    for d, a, b in peers:
        pl.semaphore_signal(barrier, inc=1, device_id=at(a, b, d), device_id_type=MESH)
    pl.semaphore_wait(barrier, len(peers))

    def remote(src, dst, ssem, rsem, dev):
        return pltpu.make_async_remote_copy(
            src_ref=src, dst_ref=dst, send_sem=ssem, recv_sem=rsem, device_id=dev, device_id_type=MESH
        )

    def halo(g, i):
        step, part, owner, start, count, where = pn.regions[i]
        return remote(
            ext.at[g, pl.ds(pn.own_at(owner) + start, count)],
            ext.at[g, pl.ds(where, count)],
            hs.at[g, i], hr.at[g, i], at(-part, -step),
        )

    def back(g, i):
        step, part, owner, start, count, where = pn.regions[i]
        return remote(
            gsend.at[g, pl.ds(where, count)],
            grecv.at[g, pl.ds(where, count)],
            gs.at[g, i], gr.at[g, i], at(part, step),
        )

    def only(cond, act):
        if cond is None:
            act()
        else:
            pl.when(cond)(act)

    def below(part):
        return None if part == 0 else (lat < nlat - 1 if part == -1 else lat > 0)

    def above(part):
        return below(-part)

    def run(make, side, ids, g, what):
        for part in (-1, 0, 1):
            chosen = [i for i in ids if pn.regions[i][1] == part]
            if chosen:
                only(side(part), lambda: [getattr(make(g, i), what)() for i in chosen] and None)

    for part in (-1, 1):
        def clear(part=part):
            for g in range(pn.groups):
                for step, p, owner, start, count, where in pn.regions:
                    if p == part:
                        ext[g, pl.ds(where, count)] = jnp.zeros((count, 2 * gw), BF16)
                    if p == -part:
                        grecv[g, pl.ds(where, count)] = jnp.zeros((count, 2 * gw), BF16)

        pl.when(lat == (0 if part == -1 else nlat - 1))(clear)

    bring(last_in).wait()
    flat = f_ref[...]
    for g in range(pn.groups):
        bring(2 * g).wait()
        bring(2 * g + 1).wait()
        for kv in range(2):
            w = wkv_ref[:, kv * qw + g * gw : kv * qw + (g + 1) * gw]
            got = jnp.dot(flat, w, preferred_element_type=F32)
            got = got.reshape(pn.rows, pn.cols // OCT, OCT, gw)
            for o in range(1, pn.octets - 1):
                ext[g, pl.ds(pn.own_at(o), pn.half), kv * gw : (kv + 1) * gw] = (
                    got[:, o - 1].reshape(pn.half, gw).astype(BF16)
                )
        run(halo, below, pn.lon_ids + pn.near_ids, g, "start")

    if pn.group_all:
        slot = dp * 4 + lat
        fall[slot] = flat

        def flip(kind):
            return ((1 - dp, lat, lon), (dp, lax.rem(lat + 2, 4), lon), (dp, lat + 1 - 2 * lax.rem(lat, 2), lon))[kind]

        def slot_of(ddp, dx):
            return (dp + ddp - 2 * dp * ddp) * 4 + lax.rem(lat + 2 * dx, 4)

        hops = [(0, 0, 0), (1, 0, 0), (2, 0, 0), (1, 1, 0), (2, 1, 0), (2, 0, 1), (2, 1, 1)]

        def hop(n):
            kind, ddp, dx = hops[n]
            s = slot_of(ddp, dx)
            return remote(fall.at[s], fall.at[s], fs.at[n], fr.at[n], flip(kind))

        def hop_in(n):
            kind, ddp, dx = hops[n]
            if kind == 0:
                s = slot_of(1 - ddp, dx)
            elif kind == 1:
                s = slot_of(ddp, 1 - dx)
            else:
                mate = lat + 1 - 2 * lax.rem(lat, 2)
                s = (dp + ddp - 2 * dp * ddp) * 4 + lax.rem(mate + 2 * dx, 4)
            return remote(fall.at[s], fall.at[s], fs.at[n], fr.at[n], flip(kind))

        for n in (0, 1, 2):
            hop(n).start()
    for n in range(last_in + 1, last_in + 5):
        bring(n).wait()

    lane = lax.broadcasted_iota(jnp.int32, (pn.nq, gw), 1)
    for g in range(pn.groups):
        got = jnp.dot(flat, wq_ref[:, g * gw : (g + 1) * gw], preferred_element_type=F32)
        dout = d_ref[:, g * gw : (g + 1) * gw].astype(F32)
        for hh in range(2):
            mine = (lane < hd) if hh == 0 else (lane >= hd)
            q2[g, hh * pn.nq : (hh + 1) * pn.nq] = jnp.where(mine, got, 0.0).astype(BF16)
            do2[g, hh * pn.nq : (hh + 1) * pn.nq] = jnp.where(mine, dout, 0.0).astype(BF16)

    nlat_all, nlon_all = valid_ref.shape

    def parts_of(n):
        shape = (pn.octets, pn.ext, OCT, n)
        o, row, c = (lax.broadcasted_iota(jnp.int32, shape, k).reshape(pn.nk, n) for k in range(3))
        return o * OCT + c, row, lax.broadcasted_iota(jnp.int32, (pn.nk, n), 1)

    col, row, li = parts_of(nlat_all)
    pick_row = jnp.where(li == row - pn.reach + lat * pn.rows, 1.0, 0.0).astype(BF16)
    col, row, li = parts_of(nlon_all)
    here = col - OCT + lon * pn.cols
    here = jnp.where(here < 0, here + nlon_all, here)
    here = jnp.where(here >= nlon_all, here - nlon_all, here)
    pick_col = li == here
    ones = jnp.ones((nlon_all, pn.nq), BF16)

    def key_values(ref):
        rows_of = jnp.dot(pick_row, ref[...].astype(F32).astype(BF16), preferred_element_type=F32)
        return jnp.dot(jnp.where(pick_col, rows_of, 0.0).astype(BF16), ones, preferred_element_type=F32)

    land = key_values(land_ref)
    ok = key_values(valid_ref)
    col, row, li = parts_of(pn.nq)
    a = row - li // pn.cols
    b = col - OCT + pn.reach - li % pn.cols
    side = 2 * pn.reach
    inside = (a >= 0) & (a <= side) & (b >= 0) & (b <= side)
    centre = (a == pn.reach) & (b == pn.reach)
    okay[...] = jnp.where(inside, jnp.where(centre, 1.0, ok), 0.0)
    per = pn.nq // pn.cols
    keys, width = pn.octets * OCT, 4 * pn.nq
    ar = lax.broadcasted_iota(jnp.int32, (16, width), 0)
    tr = lax.broadcasted_iota(jnp.int32, (16, width), 1) // pn.cols
    hot = jnp.where(ar == pn.ext - 1 - tr, 1.0, 0.0)
    spread = jnp.dot(lines_ref[...], hot, precision=lax.Precision.HIGHEST, preferred_element_type=F32)
    turn = lax.broadcasted_iota(jnp.int32, (keys, width), 1) % pn.cols
    for g in range(pn.groups):
        run(halo, above, pn.lon_ids, g, "wait_recv")
        run(halo, below, pn.corner_ids, g, "start")
        for hh in range(2):
            h = 2 * g + hh
            shifted = spread[h * keys : (h + 1) * keys]
            bit = 1
            while bit < pn.cols:
                shifted = jnp.where((turn & bit) != 0, pltpu.roll(shifted, bit, 0), shifted)
                bit *= 2
            for o in range(pn.octets):
                line = shifted[o * OCT : (o + 1) * OCT]
                for k in range(min(per, pn.ext)):
                    turned = line if k == 0 else pltpu.roll(line, width - k * pn.cols, 1)
                    for m in range((pn.ext - 1) // per + 1):
                        r = pn.ext - 1 - (m * per + k)
                        if r < 0:
                            continue
                        first = (o * pn.ext + r) * OCT
                        bias[g, first : first + OCT, hh * pn.nq : (hh + 1) * pn.nq] = (
                            turned[:, m * pn.nq : (m + 1) * pn.nq]
                            + land_bias_ref[h] * land[first : first + OCT]
                        )

    def step(g, carry):
        run(halo, above, pn.lat_ids, g, "wait_recv")
        key = ext[g, :, 0:gw]
        value = ext[g, :, gw : 2 * gw]
        qg, dg = q2[g], do2[g]
        raw = lax.dot_general(key, qg, NEAR, preferred_element_type=F32) * scale + bias[g]
        dots = lax.dot_general(value, dg, NEAR, preferred_element_type=F32)
        bent = jnp.tanh(raw * (1.0 / CAP))
        ok1 = okay[...]
        expd = jnp.exp(CAP * bent) * jnp.concatenate([ok1, ok1], axis=1)
        weight = expd * (1.0 / jnp.sum(expd, axis=0, keepdims=True))
        delta = jnp.sum(weight * dots, axis=0, keepdims=True)
        ds = (weight * (dots - delta) * ((1.0 - bent * bent) * scale)).astype(BF16)
        wb = weight.astype(BF16)
        for kv, (left, right) in enumerate(((ds, qg), (wb, dg))):
            got = jnp.dot(left, right, preferred_element_type=F32)
            for o in range(pn.octets):
                own[g, pl.ds(o * pn.half, pn.half), kv * gw : (kv + 1) * gw] = got[
                    pn.own_at(o) : pn.own_at(o) + pn.half
                ]
            gsend[g, :, kv * gw : (kv + 1) * gw] = got.astype(BF16)
        run(back, above, pn.lat_ids, g, "start")
        turned = lax.dot_general(key, ds, TALL, preferred_element_type=F32)
        both = jnp.concatenate([turned[:hd, : pn.nq], turned[hd:, pn.nq :]], axis=0)
        dq_s[g] = both.T.astype(BF16)
        return carry

    def summed(g, o, parts):
        total = own[g, pl.ds(o * pn.half, pn.half)]
        for step_, part, owner, start, count, where in pn.regions:
            if owner != o or part not in parts:
                continue
            add = grecv[g, pl.ds(where, count)].astype(F32)
            if count < pn.half:
                zero = jnp.zeros((pn.half - count, add.shape[1]), F32)
                add = jnp.concatenate([zero, add] if start else [add, zero], axis=0)
            total = total + add
        return total

    def sideways(g):
        run(back, below, pn.lat_ids, g, "wait_recv")
        for o in (0, pn.octets - 1):
            gsend[g, pl.ds(pn.own_at(o), pn.half)] = summed(g, o, (-1, 1)).astype(BF16)
        run(back, below, pn.lon_ids, g, "start")

    def kcopy(g, kv):
        to = kv * pn.groups + g
        return remote(cell.at[to], kall.at[slot], ks.at[to], kr.at[slot], (kv, g, lon))

    def kcopy_in(n):
        frm = lax.rem(slot + n, 8)
        return remote(cell.at[frm], kall.at[frm], ks.at[frm], kr.at[frm], (frm // 4, lax.rem(frm, 4), lon))

    def finish(g):
        run(back, below, pn.lon_ids, g, "wait_recv")
        halves = []
        for o in range(1, pn.octets - 1):
            halves.append(summed(g, o, (-1, 0, 1)).reshape(pn.rows, 1, OCT, 2 * gw))
        full = jnp.concatenate(halves, axis=1).reshape(pn.nq, 2 * gw).astype(BF16)
        for kv in range(2):
            cell[kv * pn.groups + g] = full[:, kv * gw : (kv + 1) * gw]
            if pn.group_all:
                pl.when(kv * pn.groups + g != slot)(lambda kv=kv: kcopy(g, kv).start())

    def later(g, carry):
        step(g, carry)
        sideways(g - 1)
        return carry

    def last(g, carry):
        later(g, carry)
        return carry

    if pn.group_all:
        step(0, 0)
        hop_in(0).wait_recv()
        for n in (3, 4):
            hop(n).start()
    else:
        step(0, 0)
    later(1, 0)
    lax.fori_loop(2, pn.groups, last, 0)
    sideways(pn.groups - 1)

    dq = jnp.concatenate([dq_s[g] for g in range(pn.groups)], axis=1)
    first = lax.dot_general(dq, wq_ref[...], NEAR, preferred_element_type=F32)
    if pn.group_all:
        fsum[...] = first
        hop_in(1).wait_recv()
        hop(5).start()
        hop_in(3).wait_recv()
        hop(6).start()
    for g in range(pn.groups):
        finish(g)
    cells = jnp.concatenate([cell[k] for k in range(2 * pn.groups)], axis=1)
    second = lax.dot_general(cells, wkv_ref[...], NEAR, preferred_element_type=F32)
    if not pn.group_all:
        cell_out[...] = cells
        fg_out[...] = (first + second).astype(BF16)
    else:
        fg_out[...] = (fsum[...] + second).astype(BF16)
        kall[slot] = cell[slot]
        for n in (2, 4, 5, 6):
            hop_in(n).wait_recv()
        for n in range(1, 8):
            kcopy_in(n).wait_recv()
        ka = kall[...].reshape(8 * pn.nq, gw)
        fa = fall[...].reshape(8 * pn.nq, fall.shape[2])
        grad = lax.dot_general(ka, fa, TALL, preferred_element_type=F32).T
        depth = grad.shape[0] // (8 * nlon)
        grad = (grad * norm).reshape(8, nlon, depth, gw)

        def zcopy(n):
            to = lax.rem(lon + n, nlon)
            return remote(zsend.at[to], zrecv.at[n - 1], zs.at[n - 1], zr.at[n - 1], (dp, lat, to))

        for z in range(nlon):
            zsend[z] = grad[:, z].reshape(8 * depth, gw).astype(BF16)
        for n in range(1, nlon):
            zcopy(n).start()
        for n in range(1, nlon):
            zcopy(n).wait_recv()
        total = zsend[lon].astype(F32)
        for n in range(1, nlon):
            total = total + zrecv[n - 1].astype(F32)
        ocol[...] = total.reshape(8, depth, gw)

        def ocopy(n, out):
            d, x = n // 4, n % 4
            tdp = lax.rem(dp + d, 2)
            tlat = lax.rem(lat + x, 4)
            frm = slot if out else tdp * 4 + lax.rem(lat + 4 - x, 4)
            where = pl.ds(pl.multiple_of(frm * gw, gw), gw)
            return remote(
                ocol.at[tdp * 4 + tlat], kv_out.at[:, where], os_.at[n], or_.at[n], (tdp, tlat, lon)
            )

        for n in range(1, 8):
            ocopy(n, True).start()
        kv_out[:, pl.ds(pl.multiple_of(slot * gw, gw), gw)] = ocol[slot]
        for n in range(1, 8):
            ocopy(n, False).wait_recv()
        for n in range(1, 8):
            kcopy_in(n).wait_send()
            ocopy(n, True).wait_send()
        for n in range(1, nlon):
            zcopy(n).wait_send()
        for n in range(7):
            hop(n).wait_send()
    for g in range(pn.groups):
        run(halo, below, pn.lon_ids + pn.lat_ids, g, "wait_send")
        run(back, above, pn.lat_ids, g, "wait_send")
        run(back, above, pn.lon_ids, g, "wait_send")


def padded_bias(position_bias, pn):
    heads, side, _ = position_bias.shape
    lead, keys = OCT - pn.reach, pn.octets * OCT
    turned = jnp.swapaxes(position_bias, 1, 2)
    turned = jnp.pad(turned, ((0, 0), (lead, keys - side - lead), (0, 16 - side)))
    return turned.reshape(heads * keys, 16)


def shards(
    fields, cotangent, query_weight, keyval_weight, position_bias, land_bias, valid_cell, land_sea
):
    rows, cols, width = fields.shape[1:]
    q_width = query_weight.shape[1]
    heads = position_bias.shape[0]
    size = q_width // heads
    reach = (position_bias.shape[1] - 1) // 2
    nlat, nlon, ndp = lax.axis_size("lat"), lax.axis_size("lon"), lax.axis_size("dp")
    pn = Plan(rows, cols, reach, heads, size, nlat, nlon, ndp)
    flat = fields.reshape(pn.nq, width)
    dout = cotangent.reshape(pn.nq, q_width)
    devices = nlat * nlon * ndp
    norm = float(pn.nq * devices) ** (-0.5)
    gw = 2 * size
    vm = pl.BlockSpec(memory_space=pltpu.VMEM)
    hbm = pl.BlockSpec(memory_space=pl.ANY)
    dma = pltpu.SemaphoreType.DMA
    nreg = len(pn.regions)
    g = pn.groups
    scratch = [
        pltpu.VMEM((g, pn.nk, 2 * gw), BF16),
        pltpu.VMEM((g, pn.nk, 2 * gw), BF16),
        pltpu.VMEM((g, pn.nk, 2 * gw), BF16),
        pltpu.VMEM((g, pn.octets * pn.half, 2 * gw), F32),
        pltpu.VMEM((g, 2 * pn.nq, gw), BF16),
        pltpu.VMEM((g, 2 * pn.nq, gw), BF16),
        pltpu.VMEM((g, pn.nk, 2 * pn.nq), F32),
        pltpu.VMEM((pn.nk, pn.nq), F32),
        pltpu.VMEM((g, pn.nq, gw), BF16),
        dma((g, nreg)), dma((g, nreg)), dma((g, nreg)), dma((g, nreg)),
        pltpu.VMEM((pn.nq, width), BF16),
        pltpu.VMEM((pn.nq, q_width), BF16),
        pltpu.VMEM(query_weight.shape, BF16),
        pltpu.VMEM(keyval_weight.shape, BF16),
        pltpu.VMEM(valid_cell.shape, jnp.int32),
        pltpu.VMEM(land_sea.shape, jnp.int32),
        pltpu.VMEM((2 * g, pn.nq, gw), BF16),
        dma((2 * g + 5,)),
    ]
    out_shape = [jax.ShapeDtypeStruct((pn.nq, width), BF16)]
    if pn.group_all:
        depth = width // devices
        out_shape.append(jax.ShapeDtypeStruct((depth, 2 * q_width), F32))
        scratch += [
            pltpu.VMEM((8, pn.nq, width), BF16),
            pltpu.VMEM((8, pn.nq, gw), BF16),
            pltpu.VMEM((nlon, 8 * depth, gw), BF16),
            pltpu.VMEM((nlon - 1, 8 * depth, gw), BF16),
            pltpu.VMEM((pn.nq, width), F32),
            pltpu.VMEM((8, depth, gw), F32),
            dma((7,)), dma((7,)), dma((8,)), dma((8,)),
            dma((nlon - 1,)), dma((nlon - 1,)), dma((8,)), dma((8,)),
        ]
    else:
        out_shape.append(jax.ShapeDtypeStruct((pn.nq, 2 * q_width), BF16))

    def kernel(*refs):
        body(pn, size ** (-0.5), norm, refs)

    field_grad, other = pl.pallas_call(
        kernel,
        out_shape=out_shape,
        in_specs=[hbm] * 4 + [vm, pl.BlockSpec(memory_space=pltpu.SMEM)] + [hbm] * 2,
        out_specs=[vm, vm],
        scratch_shapes=scratch,
        name="attention_grads",
        compiler_params=pltpu.CompilerParams(
            collective_id=0, has_side_effects=True, vmem_limit_bytes=60 * 1024 * 1024
        ),
    )(
        flat, dout, query_weight, keyval_weight, padded_bias(position_bias, pn), land_bias,
        valid_cell, land_sea,
    )
    field_grad = field_grad.reshape(1, rows, cols, width)
    if pn.group_all:
        return field_grad, other
    term = lax.dot_general(flat, other, (((0,), (0,)), ((), ())), preferred_element_type=F32)
    keyval_grad = lax.psum_scatter(
        term * norm, ("dp", "lat", "lon"), scatter_dimension=0, tiled=True
    )
    return field_grad, keyval_grad


def solution(mesh):
    block = P("dp", "lat", "lon", None)
    in_specs = (block, block, P(), P(), P(), P(), P(), P())
    out_specs = (block, P(("dp", "lat", "lon"), None))
    return jax.shard_map(shards, mesh=mesh, in_specs=in_specs, out_specs=out_specs, check_vma=False)
```
